512 devices in a mesh: inst: 8 (over z_hi, core), space: 64 (over z_lo, y, x).
Axes of the slice: x: 4, y: 8, z: 8 (z_hi: 4, z_lo: 2; z = z_hi * 2 + z_lo), core: 2. Of those that a mesh axis runs over, the one named last changes fastest.
Arguments:
- state: float32 [8, 5, 64, 32768], P('inst', None, None, 'space'), may hold values from -6 to 6
- metric: float32 [32768], P('space'), may hold values from 1 to 4
- jacobians: float32 [3, 5, 5], replicated, may hold values from -2.5 to 2.5
- dissipation: float32 [1], replicated, may hold values from 0.5 to 2
- omega: float32 [1], replicated, may hold values from 0.5 to 2
- rotor_angle: float32 [8], P('inst'), may hold values from -3.140625 to 3.140625
- counts: int32 [64], P('space'), may hold values from 384 to 512, as said below
- neighbours: int32 [6, 32768], P(None, 'space'), may hold values from 0 to 639, as said below
- mortar_pairs: int32 [8, 16384], P('inst', 'space'), may hold values from 0 to 16383, as said below
Outputs:
- updated: float32 [8, 5, 64, 32768], P('inst', None, None, 'space')
The draws below stay inside these ranges and needn't reach their ends.
Inputs may be any that keep to these rules, and one draw needn't show every extreme that they name: Some index of space has all 512 slots live; live slots are the first counts ones of a device. `neighbours`: extended numbering of a device: 64 halo slots from the previous device (its slots 64 to 127), its own 512 slots, 64 from the next device (its slots 0 to 63); every entry names a live element. `mortar_pairs`: each row is a permutation; for each instance there is one device offset, the same for all devices, such that the partners of device p's 256 faces lie on devices p plus that offset and the one after it, counted cyclically.
All inputs are finite; a program needn't handle non-finite values.
Results may differ from the reference program's by a relative error of at most 0.0001.
Values sent between devices are 32-bit elements; how exact they have to be, the bound alone decides.
A program may use at most 64 MiB of HBM per device.

```python
import math
import jax
import jax.numpy as jnp
import numpy as np
from jax import lax

FIELDS = 5
MODES = 64
E_DEV = 512
RIM = 64
MORT = 256
INSTANCES = 8
ELEMS = 32768
PLANE = 16384
N_SPACE = 64


def shared_counts(key):
    partitions = ELEMS // E_DEV
    values = jax.random.randint(jax.random.fold_in(key, 11), (partitions,), 2 * RIM + MORT, E_DEV + 1)
    busiest = jax.random.randint(jax.random.fold_in(key, 12), (), 0, partitions)
    return values.at[busiest].set(E_DEV).astype(jnp.int32)


def draw_counts(key, part):
    return shared_counts(key)


def draw_neighbours(key, part):
    per_column = jnp.repeat(shared_counts(key), E_DEV)
    upper = per_column[None, :] + 2 * RIM
    drawn = jax.random.randint(jax.random.fold_in(key, 13), (6, ELEMS), 0, upper)
    result = jnp.where(drawn < RIM + per_column[None, :], drawn, drawn - per_column[None, :] + E_DEV)
    return result.astype(jnp.int32)


def draw_mortar_pairs(key, part):
    partitions = PLANE // MORT
    faces_all = jnp.arange(PLANE, dtype=jnp.int32)
    device_shift = jax.random.randint(jax.random.fold_in(key, 21), (INSTANCES,), 0, partitions)
    chosen = jax.random.permutation(jax.random.fold_in(key, 23), INSTANCES)
    device_shift = device_shift.at[chosen[0]].set(partitions // 2)
    device_shift = device_shift.at[chosen[1]].set(partitions - 1)
    within = jax.random.randint(jax.random.fold_in(key, 24), (INSTANCES,), 1, MORT)
    offsets = (device_shift * MORT + within)[:, None]
    flips = jax.random.randint(jax.random.fold_in(key, 22), (INSTANCES, 1), 0, 4)
    return jnp.mod(jnp.bitwise_xor(faces_all[None, :], flips) + offsets, PLANE).astype(jnp.int32)


def block_scale(rng, dims, cuts, low, top_value):
    level, own = 1.0, jax.random.fold_in(rng, 6)
    for dim, blocks in cuts:
        draws = jnp.exp(jax.random.uniform(jax.random.fold_in(own, dim), (blocks,), jnp.float32, low / len(cuts), top_value / len(cuts)))
        level = level * jnp.repeat(draws, dims[dim] // blocks).reshape([-1 if axis == dim else 1 for axis in range(len(dims))])
    return level


def bell_draw(key, shape, width, reach, cuts=(), held_as=jnp.bfloat16):
    gain = block_scale(key, shape, cuts, -0.22, 0.18) if cuts else 1.0
    entries = jax.random.normal(key, shape, jnp.float32) * width * gain
    return jnp.minimum(jnp.maximum(entries, -reach), reach).astype(held_as)


def setup_inputs(seed: int = 0) -> dict:
    key_list = jax.random.split(jax.random.key(seed), 10)
    state = bell_draw(key_list[0], (INSTANCES, FIELDS, MODES, ELEMS), 1.0, 6.0, ((0, 8), (3, 64)), jnp.float32)
    metric = jnp.clip(jnp.exp(math.log(4.0) - 1.3862944 * jax.random.uniform(key_list[1], (ELEMS,), jnp.float32) ** block_scale(key_list[1], (ELEMS,), ((0, 64),), -0.2, 0.2)), 1.0, 4.0)
    jacobians = bell_draw(key_list[2], (3, FIELDS, FIELDS), FIELDS ** -0.5, 2.5, (), jnp.float32)
    dissipation = jnp.clip(jax.random.uniform(key_list[3], (1,), jnp.float32, 0.5, 2.0), 0.5, 2.0)
    omega = jnp.clip(jnp.exp(jax.random.uniform(key_list[4], (1,), jnp.float32, math.log(0.5), math.log(2.0))), 0.5, 2.0)
    rotor_angle = jnp.clip(jax.random.uniform(key_list[5], (INSTANCES,), jnp.float32, -3.140625, 3.140625), -3.140625, 3.140625)
    counts = draw_counts(jax.random.fold_in(key_list[9], 71), 0)
    neighbours = draw_neighbours(jax.random.fold_in(key_list[9], 71), 0)
    mortar_pairs = draw_mortar_pairs(jax.random.fold_in(key_list[9], 71), 0)
    return dict(state=state, metric=metric, jacobians=jacobians, dissipation=dissipation, omega=omega, rotor_angle=rotor_angle, counts=counts, neighbours=neighbours, mortar_pairs=mortar_pairs)


courant_number = 0.5

def gll_derivative():
    nodes = np.array([-1.0, -1.0 / math.sqrt(5.0), 1.0 / math.sqrt(5.0), 1.0])
    barycentric = np.array([1.0 / np.prod([nodes[j] - nodes[k] for k in range(4) if k != j]) for j in range(4)])
    derivative = np.zeros((4, 4))
    for i in range(4):
        for j in range(4):
            if i != j:
                derivative[i, j] = barycentric[j] / barycentric[i] / (nodes[i] - nodes[j])
        derivative[i, i] = -np.sum(derivative[i])
    return jnp.asarray(derivative, jnp.float32)

def spectral_matrix(inst_count, omega):
    positions = jnp.arange(inst_count)
    offset = positions[:, None] - positions[None, :]
    parity = 1.0 - 2.0 * jnp.mod(offset, 2).astype(jnp.float32)
    safe_offset = jnp.where(offset == 0, 1, offset).astype(jnp.float32)
    angle_value = jnp.pi * safe_offset / inst_count
    cot_value = 0.5 * parity / jnp.tan(angle_value)
    sine_value = jnp.sin(angle_value)
    viscous_value = parity / (2.0 * inst_count * sine_value * sine_value)
    diagonal_value = jnp.float32((inst_count * inst_count + 2.0) / (12.0 * inst_count))
    return jnp.where(offset == 0, diagonal_value, cot_value + viscous_value).astype(jnp.float32) * omega[0]

def face_trace(nodal_field, face_number):
    node_index = 3 * (face_number % 2)
    trace_block = lax.index_in_dim(nodal_field, node_index, 2 + face_number // 2, keepdims=False)
    return trace_block.reshape(trace_block.shape[0], trace_block.shape[1], 16, trace_block.shape[-1])

def face_add(nodal_field, face_number, face_values):
    direction = face_number // 2
    node_index = 3 * (face_number % 2)
    shaped = face_values.reshape(face_values.shape[0], face_values.shape[1], 4, 4, face_values.shape[-1])
    if direction == 0:
        return nodal_field.at[:, :, node_index].add(shaped)
    if direction == 1:
        return nodal_field.at[:, :, :, node_index].add(shaped)
    return nodal_field.at[:, :, :, :, node_index].add(shaped)

def mix_fields(jacobian, nodal_field):
    return jnp.einsum('gf,if...->ig...', jacobian, nodal_field, precision=lax.Precision.HIGHEST)

def derive(derivative, nodal_field, direction):
    product = jnp.tensordot(derivative, nodal_field, axes=([1], [2 + direction]), precision=lax.Precision.HIGHEST)
    return jnp.moveaxis(product, 0, 2 + direction)

def rotate(trace_block, angles):
    cosines = jnp.cos(angles)[:, None, None]
    sines = jnp.sin(angles)[:, None, None]
    velocity_two = trace_block[:, 2]
    velocity_three = trace_block[:, 3]
    new_two = cosines * velocity_two - sines * velocity_three
    new_three = sines * velocity_two + cosines * velocity_three
    return jnp.concatenate([trace_block[:, :2], new_two[:, None], new_three[:, None], trace_block[:, 4:]], axis=1)

def reference(state, metric, jacobians, dissipation, omega, rotor_angle, counts, neighbours, mortar_pairs):
    inst_count = state.shape[0]
    columns_all = state.shape[-1]
    nodal_field = state.reshape(inst_count, 5, 4, 4, 4, columns_all)
    derivative = gll_derivative()
    volume = derive(derivative, mix_fields(jacobians[0], nodal_field), 0)
    volume = volume + derive(derivative, mix_fields(jacobians[1], nodal_field), 1)
    volume = volume + derive(derivative, mix_fields(jacobians[2], nodal_field), 2)
    tendency = -metric * volume
    columns = jnp.arange(columns_all, dtype=jnp.int32)
    owners = columns // E_DEV
    positions = columns % E_DEV
    for face_number in range(6):
        neighbour_index = neighbours[face_number]
        prev_col = jnp.mod(owners - 1, N_SPACE) * E_DEV + RIM + neighbour_index
        own_col = owners * E_DEV + neighbour_index - RIM
        next_col = jnp.mod(owners + 1, N_SPACE) * E_DEV + neighbour_index - RIM - E_DEV
        source = jnp.where(neighbour_index < RIM, prev_col, jnp.where(neighbour_index < RIM + E_DEV, own_col, next_col)).astype(jnp.int32)
        inner_trace = face_trace(nodal_field, face_number)
        opposite = face_trace(nodal_field, face_number ^ 1)
        outer_trace = jnp.take(opposite, source, axis=3)
        if face_number == 5:
            interface = (positions >= 2 * RIM) & (positions < 2 * RIM + MORT)
            plane_index = jnp.where(interface, owners * MORT + positions - 2 * RIM, 0).astype(jnp.int32)
            partner = jnp.take(mortar_pairs, plane_index, axis=1)
            partner_col = (partner // MORT * E_DEV + 2 * RIM + partner % MORT).astype(jnp.int32)
            rotor_trace = jnp.take_along_axis(opposite, partner_col[:, None, None, :], axis=3)
            rotor_trace = rotate(rotor_trace, rotor_angle)
            outer_trace = jnp.where(interface[None, None, None, :], rotor_trace, outer_trace)
        normal_sign = 1.0 if face_number % 2 else -1.0
        jump_value = inner_trace - outer_trace
        flux_term = 0.5 * (normal_sign * mix_fields(jacobians[face_number // 2], jump_value) - dissipation[0] * jump_value)
        tendency = face_add(tendency, face_number, 6.0 * metric * flux_term)
    coupling = jnp.einsum('ij,j...->i...', spectral_matrix(inst_count, omega), state, precision=lax.Precision.HIGHEST)
    pseudo_step = courant_number / (metric * dissipation[0] + omega[0])
    result = state + pseudo_step * (tendency.reshape(state.shape) - coupling)
    live_mask = positions < jnp.take(counts, owners)
    return jnp.where(live_mask, result, jnp.float32(0.0))
```

```python
import functools
import math

import jax
import jax.numpy as jnp
import numpy as np
from jax import lax
from jax.experimental import pallas as pl
from jax.experimental.pallas import tpu as pltpu
from jax.sharding import PartitionSpec as P

RIM = 64
MORT = 256
ROWS = 320
ELS = 512
PIECES = 10
PIECE = ROWS // PIECES
MESH = pl.DeviceIdType.MESH
f32 = jnp.float32
bf16 = jnp.bfloat16

courant_number = 0.5


def gll_table():
    nodes = np.array([-1.0, -1.0 / math.sqrt(5.0), 1.0 / math.sqrt(5.0), 1.0])
    barycentric = np.array(
        [1.0 / np.prod([nodes[j] - nodes[k] for k in range(4) if k != j]) for j in range(4)]
    )
    derivative = np.zeros((4, 4))
    for i in range(4):
        for j in range(4):
            if i != j:
                derivative[i, j] = barycentric[j] / barycentric[i] / (nodes[i] - nodes[j])
        derivative[i, i] = -np.sum(derivative[i])
    return derivative


def node_operator():
    along = -gll_table()
    along[0, 0] -= 3.0
    along[3, 3] += 3.0
    eye = np.eye(4)
    full = np.concatenate(
        [
            np.kron(np.kron(along, eye), eye),
            np.kron(np.kron(eye, along), eye),
            np.kron(np.kron(eye, eye), along),
        ],
        axis=1,
    ).astype(np.float32)
    high = full.astype(jnp.bfloat16)
    low = (full - high.astype(np.float32)).astype(jnp.bfloat16)
    return np.concatenate([high, high, low], axis=1)


def spectral_blocks():
    count = 8

    def entry(k):
        k = k % count
        if k == 0:
            return (count * count + 2.0) / (12.0 * count)
        parity = (-1.0) ** k
        angle = math.pi * k / count
        return 0.5 * parity / math.tan(angle) + parity / (2.0 * count * math.sin(angle) ** 2)

    return [np.array([[entry(2 * d + r - s) for s in range(2)] for r in range(2)]) for d in range(4)]


def coding():
    own, near, far, back = spectral_blocks()
    turn = np.array([[0.0, -1.0], [1.0, 0.0]])

    def gap(w):
        a, b = w[:2], w[2:]
        return (near @ turn @ np.outer(a, a) - back @ turn @ np.outer(b, b) - far).ravel()

    w = np.array([0.03903, -0.69895, -1.57892, 0.64467])
    for _ in range(30):
        slope = np.stack([(gap(w + h) - gap(w - h)) / 2e-5 for h in 1e-5 * np.eye(4)], axis=1)
        w = w - np.linalg.solve(slope, gap(w))
    assert np.abs(gap(w)).max() < 1e-12
    sides = []
    for part, block, sign in ((w[:2], near, 1.0), (w[2:], back, -1.0)):
        u = part / np.linalg.norm(part)
        v = turn @ u
        sides.append((u, v, sign * float(part @ part), block @ np.linalg.inv(np.stack([u, v]))))
    table = {}
    for core, (u, v, k, mix) in enumerate(sides):
        table[core] = dict(
            mo=u[core], mp=u[1 - core], no=v[core], np=v[1 - core], k=k,
            em=mix[1 - core, 0], en=mix[1 - core, 1],
            bo=own[core, core], bp=own[core, 1 - core],
            fm=mix[core, 0], fn=mix[core, 1],
        )
    return table


def split(value):
    high = value.astype(bf16)
    low = (value - high.astype(f32)).astype(bf16)
    return high, low


def kernel(
    x_hbm, met, jac, diss, om, ang, nb, mp, dcat, out,
    X, XP, MS, MR, NS, NR, ES, ER, ACC, X4, ACC4, SA, SB, RA, RB, H,
    T, TZ, V, VU, VD, W, WU, WD, U, UX, Q, QN,
    in_sem, in4_sem, ex_s, ex_r, m_s, m_r, n_s, n_r, e_s, e_r, h_s, h_r, c_s, c_r,
):
    me = lax.axis_index("inst")
    sp = lax.axis_index("space")
    core = lax.rem(me, 2)
    mate = me + 1 - 2 * core
    ahead = lax.rem(me + 10 - 4 * core, 8)
    behind = lax.rem(me + 6 + 4 * core, 8)
    xs = lax.rem(sp, 4)
    ys = lax.rem(sp // 4, 8)
    zs = sp // 32
    nxt = lax.rem(sp + 1, 64)
    prv = lax.rem(sp + 63, 64)

    def at(z, y, x):
        return z * 32 + lax.rem(y + 8, 8) * 4 + lax.rem(x + 4, 4)

    across = at(1 - zs, ys, xs)
    y_up, y_dn = at(zs, ys + 1, xs), at(zs, ys - 1, xs)
    y_up3, y_dn3 = at(zs, ys + 3, xs), at(zs, ys - 3, xs)
    x_other = [at(zs, ys, xs + s) for s in (1, 2, 3)]

    def to(i, s):
        return {"inst": i, "space": s}

    load = pltpu.make_async_copy(x_hbm, X, in_sem)
    load.start()
    loads = [
        pltpu.make_async_copy(x_hbm.at[:, 128 * j : 128 * j + 128], X4.at[j], in4_sem.at[j]) for j in range(4)
    ]
    for copy in loads:
        copy.start()
    barrier = pltpu.get_barrier_semaphore()
    peers = [(mate, sp), (ahead, sp), (behind, sp)]
    peers += [(me, s) for s in (nxt, prv, across, y_up, y_dn, y_up3, y_dn3, *x_other)]
    for i, s in peers:
        pl.semaphore_signal(barrier, inc=1, device_id=to(i, s), device_id_type=MESH)
    pl.semaphore_wait(barrier, len(peers))
    load.wait()
    for copy in loads:
        copy.wait()

    def remote(src, dst, ss, rs, i, s):
        return pltpu.make_async_remote_copy(
            src_ref=src, dst_ref=dst, send_sem=ss, recv_sem=rs, device_id=to(i, s), device_id_type=MESH
        )

    def rows(k):
        return pl.ds(pl.multiple_of(k * PIECE, PIECE), PIECE)

    def ex(k):
        return remote(X.at[rows(k)], XP.at[rows(k)], ex_s.at[k], ex_r.at[k], mate, sp)

    def mm(k):
        return remote(MS.at[rows(k)], MR.at[rows(k)], m_s.at[k], m_r.at[k], ahead, sp)

    def nn(k):
        return remote(NS.at[rows(k)], NR.at[rows(k)], n_s.at[k], n_r.at[k], ahead, sp)

    def ee(k):
        return remote(ES.at[rows(k)], ER.at[rows(k)], e_s.at[k], e_r.at[k], mate, sp)

    table = coding()

    def coef(name):
        return jnp.where(core == 0, f32(table[0][name]), f32(table[1][name]))

    @pl.loop(0, PIECES)
    def _(k):
        ex(k).start()

    for j in range(2):
        T[:, 128 * j : 128 * j + 128] = X4[1 + j, pl.ds(0, 80, stride=4), :]
    lane = lax.broadcasted_iota(jnp.int32, (160, 128), 1)
    top, low = X[0:160, 0:128], X[160:320, 0:128]
    SA[...] = jnp.where(lane < 64, top, pltpu.roll(low, 64, 1))
    SB[...] = jnp.where(lane < 64, pltpu.roll(top, 64, 1), low)

    def stage(src, dst, slot, s):
        return remote(src, dst, c_s.at[slot], c_r.at[slot], me, s)

    hops = [
        stage(T, TZ, 0, across),
        stage(V, VD, 1, y_up), stage(V, VU, 2, y_dn),
        stage(W, WD, 3, y_up3), stage(W, WU, 4, y_dn3),
        *[stage(U, UX.at[j], 5 + j, x_other[2 - j]) for j in range(3)],
        stage(Q, QN, 8, prv),
    ]
    halo_a = remote(SA, RA, h_s.at[0], h_r.at[0], me, prv)
    halo_b = remote(SB, RB, h_s.at[1], h_r.at[1], me, nxt)

    mo, mp_ = coef("mo"), coef("mp")

    @pl.loop(0, PIECES)
    def _(k):
        ex(k).wait_recv()
        MS[rows(k)] = mo * X[rows(k)] + mp_ * XP[rows(k)]

        @pl.when(k > 0)
        def _():
            mm(jnp.maximum(k - 1, 0)).start()

        @pl.when(k == 1)
        def _():
            hops[0].start()

    halo_a.start()
    halo_b.start()
    mm(PIECES - 1).start()

    pairs = mp[...]
    rel = jnp.bitwise_and(jnp.right_shift(pairs, 8) - sp + 64, 63)
    first = rel[:, 0:1]
    below = jnp.bitwise_and(first + 63, 63)
    found = jnp.max(jnp.where(rel == below, 1, 0), axis=1, keepdims=True)
    off = jnp.where(found > 0, below, first)
    offs = jnp.broadcast_to(off, (80, MORT))
    ox = jnp.bitwise_and(offs, 3)
    oy = jnp.bitwise_and(jnp.right_shift(offs, 2), 7)
    oz = jnp.right_shift(offs, 5)
    shift = oy + jnp.where(xs < ox, 1, 0)
    flip = jnp.bitwise_and(oz + jnp.where(ys < shift, 1, 0), 1)
    short = jnp.bitwise_and(shift, 7)
    short = jnp.where(short > 4, short - 8, short)
    by3 = jnp.where(short >= 2, 1, jnp.where(short <= -2, -1, 0))
    by1 = short - 3 * by3

    hops[0].wait_recv()
    V[...] = jnp.where(flip == 1, TZ[...], T[...])

    dm = diss[0]
    node = lax.broadcasted_iota(jnp.int32, (64, ELS), 0)

    def ends(i):
        return jnp.where(jnp.bitwise_and(i + 1, 3) < 2, 1.0, 0.0)

    drag = (-3.0 * dm) * (ends(jnp.right_shift(node, 4)) + ends(jnp.right_shift(node, 2)) + ends(node))

    @pl.loop(0, 5)
    def _(g):
        highs, lows = [], []
        for d in range(3):
            mixed = jac[d, g, 0] * X[0:64]
            for h in range(1, 5):
                mixed += jac[d, g, h] * X[64 * h : 64 * h + 64]
            high, low = split(mixed)
            highs.append(high)
            lows.append(low)
        stack = jnp.concatenate(highs + lows + highs, axis=0)
        mine = pl.ds(pl.multiple_of(g * 64, 64), 64)
        ACC[mine] = jnp.dot(dcat[...], stack, preferred_element_type=f32) + drag * X[mine]

        @pl.when(g == 0)
        def _():
            hops[1].start()
            hops[2].start()

    no, np_, kk = coef("no"), coef("np"), coef("k")

    def relay(lo, hi):
        @pl.loop(lo, hi)
        def _(k):
            mm(k).wait_recv()
            NS[rows(k)] = no * X[rows(k)] + np_ * XP[rows(k)] + kk * MR[rows(k)]

            @pl.when(k > 0)
            def _():
                nn(jnp.maximum(k - 1, 0)).start()

    hops[1].wait_recv()
    hops[2].wait_recv()
    W[...] = jnp.where(by1 == 1, VU[...], jnp.where(by1 == -1, VD[...], V[...]))
    relay(0, 3)
    hops[3].start()
    hops[4].start()

    halo_a.wait_recv()
    halo_b.wait_recv()
    H[0:160] = jnp.where(lane < 64, RB[...], pltpu.roll(RA[...], 64, 1))
    H[160:320] = jnp.where(lane < 64, pltpu.roll(RB[...], 64, 1), RA[...])

    ACC4[...] = jnp.zeros_like(ACC4)
    column = lax.broadcasted_iota(jnp.int32, (640, ELS), 0)

    def mix(face, outer, g):
        d, sign = face // 2, (1.0 if face % 2 else -1.0)
        total = (3.0 * dm) * outer[g]
        for h in range(5):
            total -= (3.0 * sign) * jac[d, g, h] * outer[h]
        return total

    def gather_face(face):
        d, end = face // 2, 3 * (face % 2)
        far = 3 - end

        def pick(ref):
            if d == 0:
                return jnp.concatenate([ref[64 * g + 16 * far : 64 * g + 16 * far + 16] for g in range(5)], axis=0)
            if d == 1:
                t = 8 * (far // 2)
                return jnp.concatenate([ref[16 * a + t : 16 * a + t + 8] for a in range(20)], axis=0)

        if d == 2:
            picked = [X4[j, pl.ds(far, 80, stride=4), :] for j in range(4)] + [H[pl.ds(far, 80, stride=4), :]]
        else:
            picked = [pick(X), pick(H)]
        source = jnp.concatenate(picked, axis=1)
        high, low = split(source)
        k = nb[face : face + 1, :]
        place = jnp.where(k < RIM, k + ELS, jnp.where(k < RIM + ELS, k - RIM, k))
        if face == 5:
            q = lax.broadcasted_iota(jnp.int32, (1, ELS), 1)
            place = jnp.where((q >= 2 * RIM) & (q < 2 * RIM + MORT), -1, place)
        hot = jnp.where(column == place, 1.0, 0.0).astype(bf16)
        both = jnp.dot(jnp.concatenate([high, low], axis=0), hot, preferred_element_type=f32)
        count = source.shape[0]
        got = both[:count] + both[count:]
        per = count // 5
        outer = [got[per * h : per * h + per] for h in range(5)]
        for g in range(5):
            part = mix(face, outer, g)
            if d == 0:
                ACC[64 * g + 16 * end : 64 * g + 16 * end + 16] += part
            elif d == 1:
                sub = lax.broadcasted_iota(jnp.int32, (8, ELS), 0)
                t = 8 * (end // 2)
                keep = (sub >= 4) if end == 3 else (sub < 4)
                for a in range(4):
                    piece = pltpu.roll(part[8 * a : 8 * a + 8], 4, 0)
                    at_row = 64 * g + 16 * a + t
                    ACC[at_row : at_row + 8] += jnp.where(keep, piece, 0.0)
            else:
                for j in range(4):
                    ACC4[j, pl.ds(64 * g + end, 16, stride=4), :] = part[:, 128 * j : 128 * j + 128]

    gather_face(0)
    relay(3, 6)
    gather_face(1)
    hops[3].wait_recv()
    hops[4].wait_recv()
    U[...] = jnp.where(by3 == 1, WU[...], jnp.where(by3 == -1, WD[...], W[...]))
    gather_face(2)
    for j in range(3):
        hops[5 + j].start()
    relay(6, PIECES)
    gather_face(3)
    nn(PIECES - 1).start()
    for j in range(3):
        hops[5 + j].wait_recv()
    Q[...] = jnp.where(ox == 0, U[...], jnp.where(ox == 1, UX[0], jnp.where(ox == 2, UX[1], UX[2])))
    gather_face(4)
    hops[8].start()
    gather_face(5)

    hops[8].wait_recv()
    window = jnp.concatenate([Q[...], QN[...]], axis=1)
    high, low = split(window)
    index = jnp.bitwise_and(rel - off + 64, 63) * MORT + jnp.bitwise_and(pairs, MORT - 1)
    hot = jnp.where(lax.broadcasted_iota(jnp.int32, (2 * MORT, MORT), 0) == index, 1.0, 0.0).astype(bf16)
    both = jnp.dot(jnp.concatenate([high, low], axis=0), hot, preferred_element_type=f32)
    got = both[:80] + both[80:]
    outer = [got[16 * h : 16 * h + 16] for h in range(5)]
    turn = jnp.full((16, MORT), ang[0], f32)
    cosine, sine = jnp.cos(turn), jnp.sin(turn)
    outer[2], outer[3] = cosine * outer[2] - sine * outer[3], sine * outer[2] + cosine * outer[3]
    for g in range(5):
        part = mix(5, outer, g)
        for j in range(2):
            ACC4[1 + j, pl.ds(64 * g + 3, 16, stride=4), :] += part[:, 128 * j : 128 * j + 128]

    metric = met[...]
    w0 = om[0]
    pace = courant_number / (metric * dm + w0)
    gain = pace * metric
    drop = pace * w0
    bo, bp, fm, fn, em, en = [coef(c) for c in ("bo", "bp", "fm", "fn", "em", "en")]

    @pl.loop(0, PIECES)
    def _(k):
        r = rows(k)
        face = jnp.concatenate([ACC4[j, r] for j in range(4)], axis=1)
        ACC[r] = X[r] + gain * (ACC[r] + face) - drop * (bo * X[r] + bp * XP[r] + fm * MR[r])

    def finish(k):
        ee(k).wait_recv()
        r = rows(k)
        out[r] = ACC[r] - drop * (fn * NR[r] + ER[r])

    @pl.loop(0, PIECES)
    def _(k):
        nn(k).wait_recv()
        r = rows(k)
        ES[r] = em * MR[r] + en * NR[r]

        @pl.when(k > 0)
        def _():
            finish(jnp.maximum(k - 1, 0))

        ee(k).start()

    finish(PIECES - 1)

    @pl.loop(0, PIECES)
    def _(k):
        for copy in (ex, mm, nn, ee):
            copy(k).wait_send()

    for copy in (*hops, halo_a, halo_b):
        copy.wait_send()


def shards(state, metric, jacobians, dissipation, omega, rotor_angle, counts, neighbours, mortar_pairs):
    vmem = pl.BlockSpec(memory_space=pltpu.VMEM)
    smem = pl.BlockSpec(memory_space=pltpu.SMEM)
    whole = pltpu.VMEM((ROWS, ELS), f32)
    half = pltpu.VMEM((160, 128), f32)
    trace = pltpu.VMEM((80, MORT), f32)
    sem = pltpu.SemaphoreType.DMA
    result = pl.pallas_call(
        kernel,
        out_shape=jax.ShapeDtypeStruct((ROWS, ELS), f32),
        in_specs=[pl.BlockSpec(memory_space=pl.ANY), vmem, smem, smem, smem, smem, vmem, vmem, vmem],
        out_specs=vmem,
        scratch_shapes=[whole] * 9
        + [pltpu.VMEM((4, ROWS, 128), f32)] * 2
        + [half] * 4
        + [pltpu.VMEM((ROWS, 128), f32)]
        + [trace] * 9
        + [pltpu.VMEM((3, 80, MORT), f32)]
        + [trace] * 2
        + [sem(()), sem((4,))]
        + [sem((PIECES,))] * 8
        + [sem((2,))] * 2
        + [sem((9,))] * 2,
        compiler_params=pltpu.CompilerParams(collective_id=0, has_side_effects=True),
        name="step",
    )(
        state.reshape(ROWS, ELS),
        metric.reshape(1, ELS),
        jacobians,
        dissipation,
        omega,
        rotor_angle,
        neighbours,
        mortar_pairs,
        jnp.asarray(node_operator()),
    )
    live = jnp.arange(ELS, dtype=jnp.int32) < counts[0]
    return jnp.where(live, result.reshape(state.shape), jnp.float32(0.0))


def solution(mesh):
    return jax.shard_map(
        shards,
        mesh=mesh,
        in_specs=(
            P("inst", None, None, "space"),
            P("space"),
            P(),
            P(),
            P(),
            P("inst"),
            P("space"),
            P(None, "space"),
            P("inst", "space"),
        ),
        out_specs=P("inst", None, None, "space"),
        check_vma=False,
    )
```

```python
import functools
import math

import jax
import jax.numpy as jnp
import numpy as np
from jax import lax
from jax.experimental import pallas as pl
from jax.experimental.pallas import tpu as pltpu
from jax.sharding import PartitionSpec as P

RIM = 64
MORT = 256
ROWS = 320
ELS = 512
STEPS = 5
PIECE = ROWS // 2 // STEPS
VMEM_BYTES = 24 * 2**20
MESH = pl.DeviceIdType.MESH
f32 = jnp.float32
bf16 = jnp.bfloat16

courant_number = 0.5


def gll_table():
    nodes = np.array([-1.0, -1.0 / math.sqrt(5.0), 1.0 / math.sqrt(5.0), 1.0])
    barycentric = np.array(
        [1.0 / np.prod([nodes[j] - nodes[k] for k in range(4) if k != j]) for j in range(4)]
    )
    derivative = np.zeros((4, 4))
    for i in range(4):
        for j in range(4):
            if i != j:
                derivative[i, j] = barycentric[j] / barycentric[i] / (nodes[i] - nodes[j])
        derivative[i, i] = -np.sum(derivative[i])
    return derivative


def node_operator():
    along = -gll_table()
    along[0, 0] -= 3.0
    along[3, 3] += 3.0
    eye = np.eye(4)
    full = np.concatenate(
        [
            np.kron(np.kron(along, eye), eye),
            np.kron(np.kron(eye, along), eye),
            np.kron(np.kron(eye, eye), along),
        ],
        axis=1,
    ).astype(np.float32)
    high = full.astype(jnp.bfloat16)
    low = (full - high.astype(np.float32)).astype(jnp.bfloat16)
    return np.concatenate([high, high, low], axis=1)


def spectral_blocks():
    count = 8

    def entry(k):
        k = k % count
        if k == 0:
            return (count * count + 2.0) / (12.0 * count)
        parity = (-1.0) ** k
        angle = math.pi * k / count
        return 0.5 * parity / math.tan(angle) + parity / (2.0 * count * math.sin(angle) ** 2)

    return [np.array([[entry(2 * d + r - s) for s in range(2)] for r in range(2)]) for d in range(4)]


def coding():
    own, near, far, back = spectral_blocks()
    turn = np.array([[0.0, -1.0], [1.0, 0.0]])

    def gap(w):
        a, b = w[:2], w[2:]
        return (near @ turn @ np.outer(a, a) - back @ turn @ np.outer(b, b) - far).ravel()

    w = np.array([0.03903, -0.69895, -1.57892, 0.64467])
    for _ in range(30):
        slope = np.stack([(gap(w + h) - gap(w - h)) / 2e-5 for h in 1e-5 * np.eye(4)], axis=1)
        w = w - np.linalg.solve(slope, gap(w))
    assert np.abs(gap(w)).max() < 1e-12
    sides = []
    for part, block, sign in ((w[:2], near, 1.0), (w[2:], back, -1.0)):
        u = part / np.linalg.norm(part)
        v = turn @ u
        sides.append((u, v, sign * float(part @ part), block @ np.linalg.inv(np.stack([u, v]))))
    table = [[], []]
    for side, (u, v, k, mix) in enumerate(sides):
        for core in range(2):
            table[side].append(dict(
                mo=u[core], mp=u[1 - core], no=v[core], np=v[1 - core], k=k,
                em=mix[1 - core, 0], en=mix[1 - core, 1],
                bo=own[core, core], bp=own[core, 1 - core],
                fm=mix[core, 0], fn=mix[core, 1],
            ))
    return table


def split(value):
    high = value.astype(bf16)
    low = (value - high.astype(f32)).astype(bf16)
    return high, low


def kernel(
    x_hbm, met_hbm, jac_hbm, diss_hbm, om_hbm, ang_hbm, cnt_hbm, nb_hbm, mp_hbm, dcat_hbm, out,
    X, XP, MS, MR, NS, NR, ES, ER, ACC, X4, ACC4, SA, SB, RA, RB, H,
    T, TZ, V, VU, VD, W, WU, WD, U, UX, Q, QN,
    met, nb, mp, dcat, jac, diss, om, ang, cnt,
    in_sem, ex_s, ex_r, m_s, m_r, n_s, n_r, e_s, e_r, h_s, h_r, c_s, c_r,
):
    me = lax.axis_index("inst")
    sp = lax.axis_index("space")
    core = lax.rem(me, 2)
    mate = me + 1 - 2 * core
    up = lax.rem(me + 2, 8)
    down = lax.rem(me + 6, 8)
    xs = lax.rem(sp, 4)
    ys = lax.rem(sp // 4, 8)
    zs = sp // 32
    nxt = lax.rem(sp + 1, 64)
    prv = lax.rem(sp + 63, 64)

    def at(z, y, x):
        return z * 32 + lax.rem(y + 8, 8) * 4 + lax.rem(x + 4, 4)

    across = at(1 - zs, ys, xs)
    y_up, y_dn = at(zs, ys + 1, xs), at(zs, ys - 1, xs)
    y_up3, y_dn3 = at(zs, ys + 3, xs), at(zs, ys - 3, xs)
    x_other = [at(zs, ys, xs + s) for s in (1, 2, 3)]

    def to(i, s):
        return {"inst": i, "space": s}

    barrier = pltpu.get_barrier_semaphore()
    peers = [(mate, sp), (up, sp), (down, sp)]
    peers += [(me, s) for s in (nxt, prv, across, y_up, y_dn, y_up3, y_dn3, *x_other)]
    for i, s in peers:
        pl.semaphore_signal(barrier, inc=1, device_id=to(i, s), device_id_type=MESH)
    pairs_in = [(x_hbm, X)]
    pairs_in += [(x_hbm.at[:, 128 * j : 128 * j + 128], X4.at[j]) for j in range(4)]
    pairs_in += [
        (jac_hbm, jac), (diss_hbm, diss), (mp_hbm, mp), (dcat_hbm, dcat), (nb_hbm, nb),
        (om_hbm, om), (ang_hbm, ang), (cnt_hbm, cnt), (met_hbm, met),
    ]
    loads = [pltpu.make_async_copy(a, b, in_sem.at[j]) for j, (a, b) in enumerate(pairs_in)]
    for copy in loads:
        copy.start()
    for copy in loads:
        copy.wait()

    for j in range(2):
        T[:, 128 * j : 128 * j + 128] = X4[1 + j, pl.ds(0, 80, stride=4), :]
    lane = lax.broadcasted_iota(jnp.int32, (160, 128), 1)
    top, low = X[0:160, 0:128], X[160:320, 0:128]
    SA[...] = jnp.where(lane < 64, top, pltpu.roll(low, 64, 1))
    SB[...] = jnp.where(lane < 64, pltpu.roll(top, 64, 1), low)

    def remote(src, dst, ss, rs, i, s):
        return pltpu.make_async_remote_copy(
            src_ref=src, dst_ref=dst, send_sem=ss, recv_sem=rs, device_id=to(i, s), device_id_type=MESH
        )

    def half(side):
        return jnp.bitwise_xor(core, side) * (ROWS // 2)

    def rows(side, k):
        return pl.ds(pl.multiple_of(half(side) + k * PIECE, PIECE), PIECE)

    def flow(a, b, ss, rs, device):
        def piece(side, k):
            r = rows(side, k)
            target = mate if device is None else device[side]
            return remote(a.at[r], b.at[r], ss.at[side], rs.at[side, k], target, sp)

        def all_sent(side):
            r = pl.ds(pl.multiple_of(half(side), PIECE), ROWS // 2)
            target = mate if device is None else device[side]
            return remote(a.at[r], b.at[r], ss.at[side], rs.at[side, 0], target, sp)

        return piece, all_sent

    def plain(k, h):
        return pl.ds(pl.multiple_of(h * (ROWS // 2) + k * PIECE, PIECE), PIECE)

    def ex(h, k):
        r = plain(k, h)
        return remote(X.at[r], XP.at[r], ex_s, ex_r.at[h, k], mate, sp)

    mm, mm_sent = flow(MS, MR, m_s, m_r, (up, down))
    nn, nn_sent = flow(NS, NR, n_s, n_r, (up, down))
    ee, ee_sent = flow(ES, ER, e_s, e_r, None)

    def stage(src, dst, slot, s):
        return remote(src, dst, c_s.at[slot], c_r.at[slot], me, s)

    hops = [
        stage(T, TZ, 0, across),
        stage(V, VD, 1, y_up), stage(V, VU, 2, y_dn),
        stage(W, WD, 3, y_up3), stage(W, WU, 4, y_dn3),
        *[stage(U, UX.at[j], 5 + j, x_other[2 - j]) for j in range(3)],
        stage(Q, QN, 8, prv),
    ]
    halo_a = remote(SA, RA, h_s.at[0], h_r.at[0], me, prv)
    halo_b = remote(SB, RB, h_s.at[1], h_r.at[1], me, nxt)

    pl.semaphore_wait(barrier, len(peers))
    hops[0].start()

    @pl.loop(0, STEPS)
    def _(k):
        for h in range(2):
            ex(h, k).start()

    table = coding()

    def coef(name, side):
        return jnp.where(core == 0, f32(table[side][0][name]), f32(table[side][1][name]))

    def combine(names, parts, side, r):
        total = coef(names[0], side) * parts[0][r]
        for name, ref in zip(names[1:], parts[1:]):
            total += coef(name, side) * ref[r]
        return total

    @pl.loop(0, STEPS)
    def _(k):
        for h in range(2):
            ex(h, k).wait_recv()
        for side in range(2):
            r = rows(side, k)
            MS[r] = combine(("mo", "mp"), (X, XP), side, r)

        @pl.when(k > 0)
        def _():
            for side in range(2):
                mm(side, jnp.maximum(k - 1, 0)).start()

    halo_a.start()
    halo_b.start()
    for side in range(2):
        mm(side, STEPS - 1).start()

    pairs = mp[...]
    rel = jnp.bitwise_and(jnp.right_shift(pairs, 8) - sp + 64, 63)
    first = rel[:, 0:1]
    below = jnp.bitwise_and(first + 63, 63)
    found = jnp.max(jnp.where(rel == below, 1, 0), axis=1, keepdims=True)
    off = jnp.where(found > 0, below, first)
    offs = jnp.broadcast_to(off, (80, MORT))
    ox = jnp.bitwise_and(offs, 3)
    oy = jnp.bitwise_and(jnp.right_shift(offs, 2), 7)
    oz = jnp.right_shift(offs, 5)
    shift = oy + jnp.where(xs < ox, 1, 0)
    flip = jnp.bitwise_and(oz + jnp.where(ys < shift, 1, 0), 1)
    short = jnp.bitwise_and(shift, 7)
    short = jnp.where(short > 4, short - 8, short)
    by3 = jnp.where(short >= 2, 1, jnp.where(short <= -2, -1, 0))
    by1 = short - 3 * by3

    dm = diss[0, 0]
    node = lax.broadcasted_iota(jnp.int32, (64, ELS), 0)

    def ends(i):
        return jnp.where(jnp.bitwise_and(i + 1, 3) < 2, 1.0, 0.0)

    drag = (-3.0 * dm) * (ends(jnp.right_shift(node, 4)) + ends(jnp.right_shift(node, 2)) + ends(node))

    @pl.loop(0, 5)
    def _(g):
        highs, lows = [], []
        for d in range(3):
            mixed = jac[g, d, 0] * X[0:64]
            for h in range(1, 5):
                mixed += jac[g, d, h] * X[64 * h : 64 * h + 64]
            high, low = split(mixed)
            highs.append(high)
            lows.append(low)
        stack = jnp.concatenate(highs + lows + highs, axis=0)
        mine = pl.ds(pl.multiple_of(g * 64, 64), 64)
        ACC[mine] = jnp.dot(dcat[...], stack, preferred_element_type=f32) + drag * X[mine]

    def relay(first_step, last_step):
        @pl.loop(first_step, last_step)
        def _(k):
            for side in range(2):
                mm(side, k).wait_recv()
                r = rows(side, k)
                NS[r] = combine(("no", "np", "k"), (X, XP, MR), side, r)

            @pl.when(k > 0)
            def _():
                for side in range(2):
                    nn(side, jnp.maximum(k - 1, 0)).start()

    hops[0].wait_recv()
    V[...] = jnp.where(flip == 1, TZ[...], T[...])
    ACC4[...] = jnp.zeros_like(ACC4)
    hops[1].start()
    hops[2].start()

    column = lax.broadcasted_iota(jnp.int32, (640, ELS), 0)

    def mix(face, outer, g):
        d, sign = face // 2, (1.0 if face % 2 else -1.0)
        total = (3.0 * dm) * outer[g]
        for h in range(5):
            total -= (3.0 * sign) * jac[g, d, h] * outer[h]
        return total

    def gather_face(face):
        d, end = face // 2, 3 * (face % 2)
        far = 3 - end

        def pick(ref):
            if d == 0:
                return jnp.concatenate([ref[64 * g + 16 * far : 64 * g + 16 * far + 16] for g in range(5)], axis=0)
            t = 8 * (far // 2)
            return jnp.concatenate([ref[16 * a + t : 16 * a + t + 8] for a in range(20)], axis=0)

        if d == 2:
            picked = [X4[j, pl.ds(far, 80, stride=4), :] for j in range(4)] + [H[pl.ds(far, 80, stride=4), :]]
        else:
            picked = [pick(X), pick(H)]
        source = jnp.concatenate(picked, axis=1)
        high, low = split(source)
        k = nb[face : face + 1, :]
        place = jnp.where(k < RIM, k + ELS, jnp.where(k < RIM + ELS, k - RIM, k))
        if face == 5:
            q = lax.broadcasted_iota(jnp.int32, (1, ELS), 1)
            place = jnp.where((q >= 2 * RIM) & (q < 2 * RIM + MORT), -1, place)
        hot = jnp.where(column == place, 1.0, 0.0).astype(bf16)
        both = jnp.dot(jnp.concatenate([high, low], axis=0), hot, preferred_element_type=f32)
        count = source.shape[0]
        got = both[:count] + both[count:]
        per = count // 5
        outer = [got[per * h : per * h + per] for h in range(5)]
        for g in range(5):
            part = mix(face, outer, g)
            if d == 0:
                ACC[64 * g + 16 * end : 64 * g + 16 * end + 16] += part
            elif d == 1:
                sub = lax.broadcasted_iota(jnp.int32, (8, ELS), 0)
                t = 8 * (end // 2)
                keep = (sub >= 4) if end == 3 else (sub < 4)
                for a in range(4):
                    piece = pltpu.roll(part[8 * a : 8 * a + 8], 4, 0)
                    at_row = 64 * g + 16 * a + t
                    ACC[at_row : at_row + 8] += jnp.where(keep, piece, 0.0)
            else:
                for j in range(4):
                    ACC4[j, pl.ds(64 * g + end, 16, stride=4), :] = part[:, 128 * j : 128 * j + 128]

    relay(0, 1)
    halo_a.wait_recv()
    halo_b.wait_recv()
    H[0:160] = jnp.where(lane < 64, RB[...], pltpu.roll(RA[...], 64, 1))
    H[160:320] = jnp.where(lane < 64, pltpu.roll(RB[...], 64, 1), RA[...])
    gather_face(0)
    gather_face(1)
    hops[1].wait_recv()
    hops[2].wait_recv()
    W[...] = jnp.where(by1 == 1, VU[...], jnp.where(by1 == -1, VD[...], V[...]))
    gather_face(2)
    hops[3].start()
    hops[4].start()
    gather_face(3)
    relay(1, STEPS)
    gather_face(4)
    for side in range(2):
        nn(side, STEPS - 1).start()
    gather_face(5)
    hops[3].wait_recv()
    hops[4].wait_recv()
    U[...] = jnp.where(by3 == 1, WU[...], jnp.where(by3 == -1, WD[...], W[...]))

    metric = met[...]
    w0 = om[0, 0]
    pace = courant_number / (metric * dm + w0)
    gain = pace * metric
    drop = pace * w0
    live = lax.broadcasted_iota(jnp.int32, (1, ELS), 1) < cnt[0, 0]
    gain = jnp.where(live, gain, 0.0)
    drop = jnp.where(live, drop, 0.0)
    keep = jnp.where(live, 1.0, 0.0)
    for j in range(3):
        hops[5 + j].start()
    remote(X, XP, ex_s, ex_r.at[0, 0], mate, sp).wait_send()
    for side in range(2):
        mm_sent(side).wait_send()
    for j in range(3):
        hops[5 + j].wait_recv()
    Q[...] = jnp.where(ox == 0, U[...], jnp.where(ox == 1, UX[0], jnp.where(ox == 2, UX[1], UX[2])))
    turn = jnp.full((16, MORT), ang[0, 0], f32)
    cosine, sine = jnp.cos(turn), jnp.sin(turn)
    index = jnp.bitwise_and(rel - off + 64, 63) * MORT + jnp.bitwise_and(pairs, MORT - 1)
    hot = jnp.where(lax.broadcasted_iota(jnp.int32, (2 * MORT, MORT), 0) == index, 1.0, 0.0).astype(bf16)
    hops[8].start()
    for copy in (*hops[:8], halo_a, halo_b):
        copy.wait_send()

    hops[8].wait_recv()
    window = jnp.concatenate([Q[...], QN[...]], axis=1)
    high, low = split(window)
    both = jnp.dot(jnp.concatenate([high, low], axis=0), hot, preferred_element_type=f32)
    got = both[:80] + both[80:]
    outer = [got[16 * h : 16 * h + 16] for h in range(5)]
    outer[2], outer[3] = cosine * outer[2] - sine * outer[3], sine * outer[2] + cosine * outer[3]
    for g in range(5):
        part = mix(5, outer, g)
        for j in range(2):
            ACC4[1 + j, pl.ds(64 * g + 3, 16, stride=4), :] += part[:, 128 * j : 128 * j + 128]

    @pl.loop(0, STEPS)
    def _(k):
        for side in range(2):
            r = rows(side, k)
            face = jnp.concatenate([ACC4[j, r] for j in range(4)], axis=1)
            ACC[r] = keep * X[r] + gain * (ACC[r] + face) - drop * combine(("bo", "bp", "fm"), (X, XP, MR), side, r)

    def finish(k):
        for side in range(2):
            ee(1 - side, k).wait_recv()
            r = rows(side, k)
            out[r] = ACC[r] - drop * (coef("fn", side) * NR[r] + ER[r])

    @pl.loop(0, STEPS)
    def _(k):
        for side in range(2):
            nn(side, k).wait_recv()
            r = rows(side, k)
            ES[r] = combine(("em", "en"), (MR, NR), side, r)

        @pl.when(k > 0)
        def _():
            finish(jnp.maximum(k - 1, 0))

        for side in range(2):
            ee(side, k).start()

    hops[8].wait_send()
    for side in range(2):
        nn_sent(side).wait_send()
    finish(STEPS - 1)
    for side in range(2):
        ee_sent(side).wait_send()


def shards(state, metric, jacobians, dissipation, omega, rotor_angle, counts, neighbours, mortar_pairs):
    anywhere = pl.BlockSpec(memory_space=pltpu.HBM)
    whole = pltpu.VMEM((ROWS, ELS), f32)
    quarter = pltpu.VMEM((160, 128), f32)
    trace = pltpu.VMEM((80, MORT), f32)
    sem = pltpu.SemaphoreType.DMA
    operands = [
        state.reshape(ROWS, ELS),
        metric.reshape(1, ELS),
        jnp.transpose(jacobians, (1, 0, 2)),
        dissipation.reshape(1, 1),
        omega.reshape(1, 1),
        rotor_angle.reshape(1, 1),
        counts.reshape(1, 1),
        neighbours,
        mortar_pairs,
        jnp.asarray(node_operator()),
    ]
    operands = [a if a.size == 1 else pltpu.with_memory_space_constraint(a, pltpu.HBM) for a in operands]
    result = pl.pallas_call(
        kernel,
        out_shape=jax.ShapeDtypeStruct((ROWS, ELS), f32),
        in_specs=[pl.BlockSpec(memory_space=pltpu.VMEM) if a.size == 1 else anywhere for a in operands],
        out_specs=pl.BlockSpec(memory_space=pltpu.VMEM),
        scratch_shapes=[whole] * 9
        + [pltpu.VMEM((4, ROWS, 128), f32)] * 2
        + [quarter] * 4
        + [pltpu.VMEM((ROWS, 128), f32)]
        + [trace] * 9
        + [pltpu.VMEM((3, 80, MORT), f32)]
        + [trace] * 2
        + [pltpu.VMEM((1, ELS), f32), pltpu.VMEM((6, ELS), jnp.int32), pltpu.VMEM((1, MORT), jnp.int32)]
        + [pltpu.VMEM((64, 576), bf16), pltpu.SMEM((5, 3, 5), f32)]
        + [pltpu.SMEM((1, 1), f32)] * 3
        + [pltpu.SMEM((1, 1), jnp.int32)]
        + [sem((14,)), sem(()), sem((2, STEPS))]
        + [sem((2,)), sem((2, STEPS))] * 3
        + [sem((2,))] * 2
        + [sem((9,))] * 2,
        compiler_params=pltpu.CompilerParams(collective_id=0, has_side_effects=True, vmem_limit_bytes=VMEM_BYTES),
        name="step",
    )(
        *operands,
    )
    return result.reshape(state.shape)


def solution(mesh):
    return jax.shard_map(
        shards,
        mesh=mesh,
        in_specs=(
            P("inst", None, None, "space"),
            P("space"),
            P(),
            P(),
            P(),
            P("inst"),
            P("space"),
            P(None, "space"),
            P("inst", "space"),
        ),
        out_specs=P("inst", None, None, "space"),
        check_vma=False,
    )
```

```python
import functools
import math

import jax
import jax.numpy as jnp
import numpy as np
from jax import lax
from jax.experimental import pallas as pl
from jax.experimental.pallas import tpu as pltpu
from jax.sharding import PartitionSpec as P

RIM = 64
MORT = 256
ROWS = 320
ELS = 512
STEPS = 5
PIECE = ROWS // 2 // STEPS
VMEM_BYTES = 24 * 2**20
MESH = pl.DeviceIdType.MESH
f32 = jnp.float32
bf16 = jnp.bfloat16

courant_number = 0.5


def gll_table():
    nodes = np.array([-1.0, -1.0 / math.sqrt(5.0), 1.0 / math.sqrt(5.0), 1.0])
    barycentric = np.array(
        [1.0 / np.prod([nodes[j] - nodes[k] for k in range(4) if k != j]) for j in range(4)]
    )
    derivative = np.zeros((4, 4))
    for i in range(4):
        for j in range(4):
            if i != j:
                derivative[i, j] = barycentric[j] / barycentric[i] / (nodes[i] - nodes[j])
        derivative[i, i] = -np.sum(derivative[i])
    return derivative


def node_operator():
    along = -gll_table()
    along[0, 0] -= 3.0
    along[3, 3] += 3.0
    eye = np.eye(4)
    full = np.concatenate(
        [
            np.kron(np.kron(along, eye), eye),
            np.kron(np.kron(eye, along), eye),
            np.kron(np.kron(eye, eye), along),
        ],
        axis=1,
    ).astype(np.float32)
    high = full.astype(jnp.bfloat16)
    low = (full - high.astype(np.float32)).astype(jnp.bfloat16)
    return np.concatenate([high, high, low], axis=1)


def spectral_blocks():
    count = 8

    def entry(k):
        k = k % count
        if k == 0:
            return (count * count + 2.0) / (12.0 * count)
        parity = (-1.0) ** k
        angle = math.pi * k / count
        return 0.5 * parity / math.tan(angle) + parity / (2.0 * count * math.sin(angle) ** 2)

    return [np.array([[entry(2 * d + r - s) for s in range(2)] for r in range(2)]) for d in range(4)]


def coding():
    own, near, far, back = spectral_blocks()
    turn = np.array([[0.0, -1.0], [1.0, 0.0]])

    def gap(w):
        a, b = w[:2], w[2:]
        return (near @ turn @ np.outer(a, a) - back @ turn @ np.outer(b, b) - far).ravel()

    w = np.array([0.03903, -0.69895, -1.57892, 0.64467])
    for _ in range(30):
        slope = np.stack([(gap(w + h) - gap(w - h)) / 2e-5 for h in 1e-5 * np.eye(4)], axis=1)
        w = w - np.linalg.solve(slope, gap(w))
    assert np.abs(gap(w)).max() < 1e-12
    sides = []
    for part, block, sign in ((w[:2], near, 1.0), (w[2:], back, -1.0)):
        u = part / np.linalg.norm(part)
        v = turn @ u
        sides.append((u, v, sign * float(part @ part), block @ np.linalg.inv(np.stack([u, v]))))
    table = [[], []]
    for side, (u, v, k, mix) in enumerate(sides):
        for core in range(2):
            table[side].append(dict(
                mo=u[core], mp=u[1 - core], no=v[core], np=v[1 - core], k=k,
                em=mix[1 - core, 0], en=mix[1 - core, 1],
                bo=own[core, core], bp=own[core, 1 - core],
                fm=mix[core, 0], fn=mix[core, 1],
            ))
    return table


def split(value):
    high = value.astype(bf16)
    low = (value - high.astype(f32)).astype(bf16)
    return high, low


def kernel(
    x_hbm, met_hbm, jac_hbm, diss_hbm, om_hbm, ang_hbm, cnt_hbm, nb_hbm, mp_hbm, dcat_hbm, out,
    X, XP, MS, MR, NS, NR, ES, ER, ACC, OUT, X4, ACC4, SA, SB, RA, RB, H,
    T, TZ, V, VU, VD, W, WU, WD, U, UX, Q, QN,
    met, nb, mp, dcat, jac, diss, om, ang, cnt,
    in_sem, ex_s, ex_r, m_s, m_r, n_s, n_r, e_s, e_r, h_s, h_r, c_s, c_r, out_sem,
):
    me = lax.axis_index("inst")
    sp = lax.axis_index("space")
    core = lax.rem(me, 2)
    mate = me + 1 - 2 * core
    up = lax.rem(me + 2, 8)
    down = lax.rem(me + 6, 8)
    xs = lax.rem(sp, 4)
    ys = lax.rem(sp // 4, 8)
    zs = sp // 32
    nxt = lax.rem(sp + 1, 64)
    prv = lax.rem(sp + 63, 64)

    def at(z, y, x):
        return z * 32 + lax.rem(y + 8, 8) * 4 + lax.rem(x + 4, 4)

    across = at(1 - zs, ys, xs)
    y_up, y_dn = at(zs, ys + 1, xs), at(zs, ys - 1, xs)
    y_up3, y_dn3 = at(zs, ys + 3, xs), at(zs, ys - 3, xs)
    x_other = [at(zs, ys, xs + s) for s in (1, 2, 3)]

    def to(i, s):
        return {"inst": i, "space": s}

    barrier = pltpu.get_barrier_semaphore()
    peers = [(mate, sp), (up, sp), (down, sp)]
    peers += [(me, s) for s in (nxt, prv, across, y_up, y_dn, y_up3, y_dn3, *x_other)]
    for i, s in peers:
        pl.semaphore_signal(barrier, inc=1, device_id=to(i, s), device_id_type=MESH)
    pairs_in = [(x_hbm.at[:, 128 * j : 128 * j + 128], X4.at[j]) for j in (1, 2)]
    pairs_in += [(x_hbm, X)]
    pairs_in += [(x_hbm.at[:, 128 * j : 128 * j + 128], X4.at[j]) for j in (0, 3)]
    pairs_in += [
        (jac_hbm, jac), (diss_hbm, diss), (mp_hbm, mp), (dcat_hbm, dcat), (nb_hbm, nb),
        (om_hbm, om), (ang_hbm, ang), (cnt_hbm, cnt), (met_hbm, met),
    ]
    loads = [pltpu.make_async_copy(a, b, in_sem.at[j]) for j, (a, b) in enumerate(pairs_in)]
    for copy in loads:
        copy.start()
    for j in range(2):
        loads[j].wait()
    for j in range(2):
        T[:, 128 * j : 128 * j + 128] = X4[1 + j, pl.ds(0, 80, stride=4), :]

    def remote(src, dst, ss, rs, i, s):
        return pltpu.make_async_remote_copy(
            src_ref=src, dst_ref=dst, send_sem=ss, recv_sem=rs, device_id=to(i, s), device_id_type=MESH
        )

    def half(side):
        return jnp.bitwise_xor(core, side) * (ROWS // 2)

    def rows(side, k):
        return pl.ds(pl.multiple_of(half(side) + k * PIECE, PIECE), PIECE)

    def flow(a, b, ss, rs, device):
        def piece(side, k):
            r = rows(side, k)
            target = mate if device is None else device[side]
            return remote(a.at[r], b.at[r], ss.at[side], rs.at[side, k], target, sp)

        def all_sent(side):
            r = pl.ds(pl.multiple_of(half(side), PIECE), ROWS // 2)
            target = mate if device is None else device[side]
            return remote(a.at[r], b.at[r], ss.at[side], rs.at[side, 0], target, sp)

        return piece, all_sent

    def plain(k, h):
        return pl.ds(pl.multiple_of(h * (ROWS // 2) + k * PIECE, PIECE), PIECE)

    def ex(h, k):
        r = plain(k, h)
        return remote(X.at[r], XP.at[r], ex_s, ex_r.at[h, k], mate, sp)

    mm, mm_sent = flow(MS, MR, m_s, m_r, (up, down))
    nn, nn_sent = flow(NS, NR, n_s, n_r, (up, down))
    ee, ee_sent = flow(ES, ER, e_s, e_r, None)

    def stage(src, dst, slot, s):
        return remote(src, dst, c_s.at[slot], c_r.at[slot], me, s)

    lo, hi = pl.ds(0, 40), pl.ds(40, 40)

    def ring(src, up_dst, dn_dst, slot, r, u, d):
        return [stage(src.at[r], dn_dst.at[r], slot, u), stage(src.at[r], up_dst.at[r], slot + 1, d)]

    def spread(src, slot, r):
        return [stage(src.at[r], UX.at[j, r], slot + j, x_other[2 - j]) for j in range(3)]

    across_hop = stage(T, TZ, 0, across)
    a1, a2 = ring(V, VU, VD, 1, lo, y_up, y_dn), ring(W, WU, WD, 3, lo, y_up3, y_dn3)
    a3 = spread(U, 5, lo)
    b1 = spread(V, 8, hi)
    b2, b3 = ring(U, VU, VD, 11, hi, y_up, y_dn), ring(W, WU, WD, 13, hi, y_up3, y_dn3)
    last_hop = stage(Q, QN, 15, prv)

    def begin(copies):
        for copy in copies:
            copy.start()

    def arrive(copies):
        for copy in copies:
            copy.wait_recv()

    halo_a = remote(SA, RA, h_s.at[0], h_r.at[0], me, prv)
    halo_b = remote(SB, RB, h_s.at[1], h_r.at[1], me, nxt)

    pl.semaphore_wait(barrier, len(peers))
    across_hop.start()
    for copy in loads[2:]:
        copy.wait()

    @pl.loop(0, STEPS)
    def _(k):
        for h in range(2):
            ex(h, k).start()

    lane = lax.broadcasted_iota(jnp.int32, (160, 128), 1)
    top, low = X4[0, 0:160], X4[0, 160:320]
    SA[...] = jnp.where(lane < 64, top, pltpu.roll(low, 64, 1))
    SB[...] = jnp.where(lane < 64, pltpu.roll(top, 64, 1), low)
    table = coding()

    def coef(name, side):
        return jnp.where(core == 0, f32(table[side][0][name]), f32(table[side][1][name]))

    def combine(names, parts, side, r):
        total = coef(names[0], side) * parts[0][r]
        for name, ref in zip(names[1:], parts[1:]):
            total += coef(name, side) * ref[r]
        return total

    @pl.loop(0, STEPS)
    def _(k):
        for h in range(2):
            ex(h, k).wait_recv()
        for side in range(2):
            r = rows(side, k)
            MS[r] = combine(("mo", "mp"), (X, XP), side, r)

        @pl.when(k > 0)
        def _():
            for side in range(2):
                mm(side, jnp.maximum(k - 1, 0)).start()

    halo_a.start()
    halo_b.start()
    for side in range(2):
        mm(side, STEPS - 1).start()

    pairs = mp[...]
    rel = jnp.bitwise_and(jnp.right_shift(pairs, 8) - sp + 64, 63)
    first = rel[:, 0:1]
    below = jnp.bitwise_and(first + 63, 63)
    found = jnp.max(jnp.where(rel == below, 1, 0), axis=1, keepdims=True)
    off = jnp.where(found > 0, below, first)
    offs = jnp.broadcast_to(off, (40, MORT))
    ox = jnp.bitwise_and(offs, 3)
    oy = jnp.bitwise_and(jnp.right_shift(offs, 2), 7)
    oz = jnp.right_shift(offs, 5)

    def y_moves(carry):
        shift = oy + jnp.where(carry, 1, 0)
        short = jnp.bitwise_and(shift, 7)
        short = jnp.where(short > 4, short - 8, short)
        by3 = jnp.where(short >= 2, 1, jnp.where(short <= -2, -1, 0))
        return shift, short - 3 * by3, by3

    shift, a_by1, a_by3 = y_moves(xs < ox)
    _, b_by1, b_by3 = y_moves(xs + ox >= 4)
    flip = jnp.bitwise_and(oz + jnp.where(ys < shift, 1, 0), 1)

    def three(move, ref, up_ref, dn_ref, r):
        return jnp.where(move == 1, up_ref[r], jnp.where(move == -1, dn_ref[r], ref[r]))

    def along_x(ref, r):
        return jnp.where(ox == 0, ref[r], jnp.where(ox == 1, UX[0, r], jnp.where(ox == 2, UX[1, r], UX[2, r])))

    dm = diss[0, 0]
    node = lax.broadcasted_iota(jnp.int32, (64, ELS), 0)

    def ends(i):
        return jnp.where(jnp.bitwise_and(i + 1, 3) < 2, 1.0, 0.0)

    drag = (-3.0 * dm) * (ends(jnp.right_shift(node, 4)) + ends(jnp.right_shift(node, 2)) + ends(node))

    @pl.loop(0, 5)
    def _(g):
        highs, lows = [], []
        for d in range(3):
            mixed = jac[g, d, 0] * X[0:64]
            for h in range(1, 5):
                mixed += jac[g, d, h] * X[64 * h : 64 * h + 64]
            high, low = split(mixed)
            highs.append(high)
            lows.append(low)
        stack = jnp.concatenate(highs + lows + highs, axis=0)
        mine = pl.ds(pl.multiple_of(g * 64, 64), 64)
        ACC[mine] = jnp.dot(dcat[...], stack, preferred_element_type=f32) + drag * X[mine]

    def relay(first_step, last_step):
        @pl.loop(first_step, last_step)
        def _(k):
            for side in range(2):
                mm(side, k).wait_recv()
                r = rows(side, k)
                NS[r] = combine(("no", "np", "k"), (X, XP, MR), side, r)

            @pl.when(k > 0)
            def _():
                for side in range(2):
                    nn(side, jnp.maximum(k - 1, 0)).start()

    arrive([across_hop])
    for r in (lo, hi):
        V[r] = jnp.where(flip == 1, TZ[r], T[r])
    ACC4[0] = jnp.zeros((ROWS, 128), f32)
    begin(b1)
    begin(a1)

    column = lax.broadcasted_iota(jnp.int32, (640, ELS), 0)

    def mix(face, outer, g):
        d, sign = face // 2, (1.0 if face % 2 else -1.0)
        total = (3.0 * dm) * outer[g]
        for h in range(5):
            total -= (3.0 * sign) * jac[g, d, h] * outer[h]
        return total

    def gather_face(face):
        d, end = face // 2, 3 * (face % 2)
        far = 3 - end

        def pick(ref):
            if d == 0:
                return jnp.concatenate([ref[64 * g + 16 * far : 64 * g + 16 * far + 16] for g in range(5)], axis=0)
            t = 8 * (far // 2)
            return jnp.concatenate([ref[16 * a + t : 16 * a + t + 8] for a in range(20)], axis=0)

        if d == 2:
            picked = [X4[j, pl.ds(far, 80, stride=4), :] for j in range(4)] + [H[pl.ds(far, 80, stride=4), :]]
        else:
            picked = [pick(X), pick(H)]
        source = jnp.concatenate(picked, axis=1)
        high, low = split(source)
        k = nb[face : face + 1, :]
        place = jnp.where(k < RIM, k + ELS, jnp.where(k < RIM + ELS, k - RIM, k))
        if face == 5:
            q = lax.broadcasted_iota(jnp.int32, (1, ELS), 1)
            place = jnp.where((q >= 2 * RIM) & (q < 2 * RIM + MORT), -1, place)
        hot = jnp.where(column == place, 1.0, 0.0).astype(bf16)
        both = jnp.dot(jnp.concatenate([high, low], axis=0), hot, preferred_element_type=f32)
        count = source.shape[0]
        got = both[:count] + both[count:]
        per = count // 5
        outer = [got[per * h : per * h + per] for h in range(5)]
        for g in range(5):
            part = mix(face, outer, g)
            if d == 0:
                ACC[64 * g + 16 * end : 64 * g + 16 * end + 16] += part
            elif d == 1:
                sub = lax.broadcasted_iota(jnp.int32, (8, ELS), 0)
                t = 8 * (end // 2)
                keep = (sub >= 4) if end == 3 else (sub < 4)
                for a in range(4):
                    piece = pltpu.roll(part[8 * a : 8 * a + 8], 4, 0)
                    at_row = 64 * g + 16 * a + t
                    ACC[at_row : at_row + 8] += jnp.where(keep, piece, 0.0)
            else:
                for j in range(4):
                    ACC4[j, pl.ds(64 * g + end, 16, stride=4), :] = part[:, 128 * j : 128 * j + 128]

    relay(0, 1)
    halo_a.wait_recv()
    halo_b.wait_recv()
    H[0:160] = jnp.where(lane < 64, RB[...], pltpu.roll(RA[...], 64, 1))
    H[160:320] = jnp.where(lane < 64, pltpu.roll(RB[...], 64, 1), RA[...])
    for j in range(1, 4):
        ACC4[j] = jnp.zeros((ROWS, 128), f32)
    gather_face(0)
    arrive(a1)
    W[lo] = three(a_by1, V, VU, VD, lo)
    gather_face(1)
    begin(a2)
    arrive(b1)
    U[hi] = along_x(V, hi)
    relay(1, 2)
    begin(b2)
    gather_face(2)
    relay(2, 4)
    gather_face(3)
    arrive(b2)
    W[hi] = three(b_by1, U, VU, VD, hi)
    relay(4, STEPS)
    begin(b3)
    gather_face(4)
    for side in range(2):
        nn(side, STEPS - 1).start()
    arrive(a2)
    U[lo] = three(a_by3, W, WU, WD, lo)
    gather_face(5)
    begin(a3)

    metric = met[...]
    w0 = om[0, 0]
    pace = courant_number / (metric * dm + w0)
    gain = pace * metric
    drop = pace * w0
    live = lax.broadcasted_iota(jnp.int32, (1, ELS), 1) < cnt[0, 0]
    gain = jnp.where(live, gain, 0.0)
    drop = jnp.where(live, drop, 0.0)
    keep = jnp.where(live, 1.0, 0.0)
    remote(X, XP, ex_s, ex_r.at[0, 0], mate, sp).wait_send()
    for side in range(2):
        mm_sent(side).wait_send()
    turn = jnp.full((16, MORT), ang[0, 0], f32)
    cosine, sine = jnp.cos(turn), jnp.sin(turn)
    index = jnp.bitwise_and(rel - off + 64, 63) * MORT + jnp.bitwise_and(pairs, MORT - 1)
    hot = jnp.where(lax.broadcasted_iota(jnp.int32, (2 * MORT, MORT), 0) == index, 1.0, 0.0).astype(bf16)
    arrive(b3)
    Q[hi] = three(b_by3, W, WU, WD, hi)
    arrive(a3)
    Q[lo] = along_x(U, lo)
    for copy in (across_hop, *a1, *a2, *b1, *b2, *b3, *a3, halo_a, halo_b):
        copy.wait_send()
    last_hop.start()
    arrive([last_hop])
    window = jnp.concatenate([Q[...], QN[...]], axis=1)
    high, low = split(window)
    both = jnp.dot(jnp.concatenate([high, low], axis=0), hot, preferred_element_type=f32)
    got = both[:80] + both[80:]
    outer = [got[16 * h : 16 * h + 16] for h in range(5)]
    outer[2], outer[3] = cosine * outer[2] - sine * outer[3], sine * outer[2] + cosine * outer[3]
    for g in range(5):
        part = mix(5, outer, g)
        for j in range(2):
            ACC4[1 + j, pl.ds(64 * g + 3, 16, stride=4), :] += part[:, 128 * j : 128 * j + 128]

    @pl.loop(0, STEPS)
    def _(k):
        for side in range(2):
            r = rows(side, k)
            face = jnp.concatenate([ACC4[j, r] for j in range(4)], axis=1)
            ACC[r] = keep * X[r] + gain * (ACC[r] + face) - drop * combine(("bo", "bp", "fm"), (X, XP, MR), side, r)

    @pl.loop(0, STEPS)
    def _(k):
        for side in range(2):
            nn(side, k).wait_recv()
            r = rows(side, k)
            ES[r] = combine(("em", "en"), (MR, NR), side, r)

        @pl.when(k > 0)
        def _():
            for side in range(2):
                ee(side, jnp.maximum(k - 1, 0)).start()

    last_hop.wait_send()
    for side in range(2):
        nn_sent(side).wait_send()
    for side in range(2):
        ee(side, STEPS - 1).start()

    def put(side, k):
        r = rows(side, k)
        return pltpu.make_async_copy(OUT.at[r], out.at[r], out_sem.at[side, k])

    @pl.loop(0, STEPS)
    def _(k):
        for side in range(2):
            ee(1 - side, k).wait_recv()
            r = rows(side, k)
            OUT[r] = ACC[r] - drop * (coef("fn", side) * NR[r] + ER[r])
            put(side, k).start()

    for side in range(2):
        ee_sent(side).wait_send()

    @pl.loop(0, STEPS)
    def _(k):
        for side in range(2):
            put(side, k).wait()


def shards(state, metric, jacobians, dissipation, omega, rotor_angle, counts, neighbours, mortar_pairs):
    anywhere = pl.BlockSpec(memory_space=pltpu.HBM)
    whole = pltpu.VMEM((ROWS, ELS), f32)
    quarter = pltpu.VMEM((160, 128), f32)
    trace = pltpu.VMEM((80, MORT), f32)
    sem = pltpu.SemaphoreType.DMA
    operands = [
        state.reshape(ROWS, ELS),
        metric.reshape(1, ELS),
        jnp.transpose(jacobians, (1, 0, 2)),
        dissipation.reshape(1, 1),
        omega.reshape(1, 1),
        rotor_angle.reshape(1, 1),
        counts.reshape(1, 1),
        neighbours,
        mortar_pairs,
        jnp.asarray(node_operator()),
    ]
    operands = [a if a.size == 1 else pltpu.with_memory_space_constraint(a, pltpu.HBM) for a in operands]
    result = pl.pallas_call(
        kernel,
        out_shape=jax.ShapeDtypeStruct((ROWS, ELS), f32),
        in_specs=[pl.BlockSpec(memory_space=pltpu.VMEM) if a.size == 1 else anywhere for a in operands],
        out_specs=pl.BlockSpec(memory_space=pl.ANY),
        scratch_shapes=[whole] * 10
        + [pltpu.VMEM((4, ROWS, 128), f32)] * 2
        + [quarter] * 4
        + [pltpu.VMEM((ROWS, 128), f32)]
        + [trace] * 9
        + [pltpu.VMEM((3, 80, MORT), f32)]
        + [trace] * 2
        + [pltpu.VMEM((1, ELS), f32), pltpu.VMEM((6, ELS), jnp.int32), pltpu.VMEM((1, MORT), jnp.int32)]
        + [pltpu.VMEM((64, 576), bf16), pltpu.SMEM((5, 3, 5), f32)]
        + [pltpu.SMEM((1, 1), f32)] * 3
        + [pltpu.SMEM((1, 1), jnp.int32)]
        + [sem((14,)), sem(()), sem((2, STEPS))]
        + [sem((2,)), sem((2, STEPS))] * 3
        + [sem((2,))] * 2
        + [sem((16,))] * 2
        + [sem((2, STEPS))],
        compiler_params=pltpu.CompilerParams(collective_id=0, has_side_effects=True, vmem_limit_bytes=VMEM_BYTES),
        name="step",
    )(
        *operands,
    )
    return result.reshape(state.shape)


def solution(mesh):
    return jax.shard_map(
        shards,
        mesh=mesh,
        in_specs=(
            P("inst", None, None, "space"),
            P("space"),
            P(),
            P(),
            P(),
            P("inst"),
            P("space"),
            P(None, "space"),
            P("inst", "space"),
        ),
        out_specs=P("inst", None, None, "space"),
        check_vma=False,
    )
```

```python
import functools
import math

import jax
import jax.numpy as jnp
import numpy as np
from jax import lax
from jax.experimental import pallas as pl
from jax.experimental.pallas import tpu as pltpu
from jax.sharding import PartitionSpec as P

RIM = 64
MORT = 256
ROWS = 320
ELS = 512
STEPS = 5
PIECE = ROWS // 2 // STEPS
VMEM_BYTES = 24 * 2**20
MESH = pl.DeviceIdType.MESH
f32 = jnp.float32
bf16 = jnp.bfloat16

courant_number = 0.5


def gll_table():
    nodes = np.array([-1.0, -1.0 / math.sqrt(5.0), 1.0 / math.sqrt(5.0), 1.0])
    barycentric = np.array(
        [1.0 / np.prod([nodes[j] - nodes[k] for k in range(4) if k != j]) for j in range(4)]
    )
    derivative = np.zeros((4, 4))
    for i in range(4):
        for j in range(4):
            if i != j:
                derivative[i, j] = barycentric[j] / barycentric[i] / (nodes[i] - nodes[j])
        derivative[i, i] = -np.sum(derivative[i])
    return derivative


def node_operator():
    along = -gll_table()
    along[0, 0] -= 3.0
    along[3, 3] += 3.0
    eye = np.eye(4)
    full = np.concatenate(
        [
            np.kron(np.kron(along, eye), eye),
            np.kron(np.kron(eye, along), eye),
            np.kron(np.kron(eye, eye), along),
        ],
        axis=1,
    ).astype(np.float32)
    high = full.astype(jnp.bfloat16)
    low = (full - high.astype(np.float32)).astype(jnp.bfloat16)
    return np.concatenate([high, high, low], axis=1)


def spectral_blocks():
    count = 8

    def entry(k):
        k = k % count
        if k == 0:
            return (count * count + 2.0) / (12.0 * count)
        parity = (-1.0) ** k
        angle = math.pi * k / count
        return 0.5 * parity / math.tan(angle) + parity / (2.0 * count * math.sin(angle) ** 2)

    return [np.array([[entry(2 * d + r - s) for s in range(2)] for r in range(2)]) for d in range(4)]


def coding():
    own, near, far, back = spectral_blocks()
    turn = np.array([[0.0, -1.0], [1.0, 0.0]])

    def gap(w):
        a, b = w[:2], w[2:]
        return (near @ turn @ np.outer(a, a) - back @ turn @ np.outer(b, b) - far).ravel()

    w = np.array([0.03903, -0.69895, -1.57892, 0.64467])
    for _ in range(30):
        slope = np.stack([(gap(w + h) - gap(w - h)) / 2e-5 for h in 1e-5 * np.eye(4)], axis=1)
        w = w - np.linalg.solve(slope, gap(w))
    assert np.abs(gap(w)).max() < 1e-12
    sides = []
    for part, block, sign in ((w[:2], near, 1.0), (w[2:], back, -1.0)):
        u = part / np.linalg.norm(part)
        v = turn @ u
        sides.append((u, v, sign * float(part @ part), block @ np.linalg.inv(np.stack([u, v]))))
    table = [[], []]
    for side, (u, v, k, mix) in enumerate(sides):
        for core in range(2):
            table[side].append(dict(
                mo=u[core], mp=u[1 - core], no=v[core], np=v[1 - core], k=k,
                em=mix[1 - core, 0], en=mix[1 - core, 1],
                bo=own[core, core], bp=own[core, 1 - core],
                fm=mix[core, 0], fn=mix[core, 1],
            ))
    return table


def split(value):
    high = value.astype(bf16)
    low = (value - high.astype(f32)).astype(bf16)
    return high, low


def kernel(
    x_hbm, met_hbm, jac_hbm, diss_hbm, om_hbm, ang_hbm, cnt_hbm, nb_hbm, mp_hbm, dcat_hbm, out,
    X, XP, MS, MR, NS, NR, ES, ER, ACC, OUT, X4, ACC4, SA, SB, RA, RB, H,
    T, TZ, V, VU, VD, W, WU, WD, U, UX, Q, QN,
    met, nb, mp, dcat, jac, diss, om, ang, cnt,
    in_sem, ex_s, ex_r, m_s, m_r, n_s, n_r, e_s, e_r, h_s, h_r, c_s, c_r, out_sem,
):
    me = lax.axis_index("inst")
    sp = lax.axis_index("space")
    core = lax.rem(me, 2)
    mate = me + 1 - 2 * core
    up = lax.rem(me + 2, 8)
    down = lax.rem(me + 6, 8)
    xs = lax.rem(sp, 4)
    ys = lax.rem(sp // 4, 8)
    zs = sp // 32
    nxt = lax.rem(sp + 1, 64)
    prv = lax.rem(sp + 63, 64)

    def at(z, y, x):
        return z * 32 + lax.rem(y + 8, 8) * 4 + lax.rem(x + 4, 4)

    across = at(1 - zs, ys, xs)
    y_up, y_dn = at(zs, ys + 1, xs), at(zs, ys - 1, xs)
    y_up3, y_dn3 = at(zs, ys + 3, xs), at(zs, ys - 3, xs)
    x_other = [at(zs, ys, xs + s) for s in (1, 2, 3)]

    def to(i, s):
        return {"inst": i, "space": s}

    barrier = pltpu.get_barrier_semaphore()
    peers = [(mate, sp), (up, sp), (down, sp)]
    peers += [(me, s) for s in (nxt, prv, across, y_up, y_dn, y_up3, y_dn3, *x_other)]
    for i, s in peers:
        pl.semaphore_signal(barrier, inc=1, device_id=to(i, s), device_id_type=MESH)
    pairs_in = [(x_hbm.at[:, 128 * j : 128 * j + 128], X4.at[j]) for j in (1, 2)]
    pairs_in += [(x_hbm, X)]
    pairs_in += [(x_hbm.at[:, 128 * j : 128 * j + 128], X4.at[j]) for j in (0, 3)]
    pairs_in += [
        (jac_hbm, jac), (diss_hbm, diss), (mp_hbm, mp), (dcat_hbm, dcat), (nb_hbm, nb),
        (om_hbm, om), (ang_hbm, ang), (cnt_hbm, cnt), (met_hbm, met),
    ]
    loads = [pltpu.make_async_copy(a, b, in_sem.at[j]) for j, (a, b) in enumerate(pairs_in)]
    for copy in loads:
        copy.start()
    for j in range(2):
        loads[j].wait()
    for j in range(2):
        T[:, 128 * j : 128 * j + 128] = X4[1 + j, pl.ds(0, 80, stride=4), :]

    def remote(src, dst, ss, rs, i, s):
        return pltpu.make_async_remote_copy(
            src_ref=src, dst_ref=dst, send_sem=ss, recv_sem=rs, device_id=to(i, s), device_id_type=MESH
        )

    def half(side):
        return jnp.bitwise_xor(core, side) * (ROWS // 2)

    def rows(side, k):
        return pl.ds(pl.multiple_of(half(side) + k * PIECE, PIECE), PIECE)

    def flow(a, b, ss, rs, device):
        def piece(side, k):
            r = rows(side, k)
            target = mate if device is None else device[side]
            return remote(a.at[r], b.at[r], ss.at[side], rs.at[side, k], target, sp)

        def all_sent(side):
            r = pl.ds(pl.multiple_of(half(side), PIECE), ROWS // 2)
            target = mate if device is None else device[side]
            return remote(a.at[r], b.at[r], ss.at[side], rs.at[side, 0], target, sp)

        return piece, all_sent

    def plain(k, h):
        return pl.ds(pl.multiple_of(h * (ROWS // 2) + k * PIECE, PIECE), PIECE)

    def ex(h, k):
        r = plain(k, h)
        return remote(X.at[r], XP.at[r], ex_s, ex_r.at[h, k], mate, sp)

    mm, mm_sent = flow(MS, MR, m_s, m_r, (up, down))
    nn, nn_sent = flow(NS, NR, n_s, n_r, (up, down))
    ee, ee_sent = flow(ES, ER, e_s, e_r, None)

    def stage(src, dst, slot, s):
        return remote(src, dst, c_s.at[slot // 15], c_r.at[slot], me, s)

    lo, hi = pl.ds(0, 40), pl.ds(40, 40)

    def ring(src, up_dst, dn_dst, slot, r, u, d):
        return [stage(src.at[r], dn_dst.at[r], slot, u), stage(src.at[r], up_dst.at[r], slot + 1, d)]

    def spread(src, slot, r):
        return [stage(src.at[r], UX.at[j, r], slot + j, x_other[2 - j]) for j in range(3)]

    across_hop = stage(T, TZ, 0, across)
    a1, a2 = ring(V, VU, VD, 1, lo, y_up, y_dn), ring(W, WU, WD, 3, lo, y_up3, y_dn3)
    a3 = spread(U, 5, lo)
    b1 = spread(V, 8, hi)
    b2, b3 = ring(U, VU, VD, 11, hi, y_up, y_dn), ring(W, WU, WD, 13, hi, y_up3, y_dn3)
    last_lo = stage(Q.at[lo], QN.at[lo], 15, prv)
    last_hi = stage(Q.at[hi], QN.at[hi], 16, prv)

    def begin(copies):
        for copy in copies:
            copy.start()

    def arrive(copies):
        for copy in copies:
            copy.wait_recv()

    halo_a = remote(SA, RA, h_s, h_r.at[0], me, prv)
    halo_b = remote(SB, RB, h_s, h_r.at[1], me, nxt)

    pl.semaphore_wait(barrier, len(peers))
    across_hop.start()
    for copy in loads[2:]:
        copy.wait()

    @pl.loop(0, STEPS)
    def _(k):
        for h in range(2):
            ex(h, k).start()

    lane = lax.broadcasted_iota(jnp.int32, (160, 128), 1)
    top, low = X4[0, 0:160], X4[0, 160:320]
    SA[...] = jnp.where(lane < 64, top, pltpu.roll(low, 64, 1))
    SB[...] = jnp.where(lane < 64, pltpu.roll(top, 64, 1), low)
    table = coding()

    def coef(name, side):
        return jnp.where(core == 0, f32(table[side][0][name]), f32(table[side][1][name]))

    def combine(names, parts, side, r):
        total = coef(names[0], side) * parts[0][r]
        for name, ref in zip(names[1:], parts[1:]):
            total += coef(name, side) * ref[r]
        return total

    @pl.loop(0, STEPS)
    def _(k):
        for h in range(2):
            ex(h, k).wait_recv()
        for side in range(2):
            r = rows(side, k)
            MS[r] = combine(("mo", "mp"), (X, XP), side, r)

        @pl.when(k > 0)
        def _():
            for side in range(2):
                mm(side, jnp.maximum(k - 1, 0)).start()

    halo_a.start()
    halo_b.start()
    for side in range(2):
        mm(side, STEPS - 1).start()

    pairs = mp[...]
    rel = jnp.bitwise_and(jnp.right_shift(pairs, 8) - sp + 64, 63)
    first = rel[:, 0:1]
    below = jnp.bitwise_and(first + 63, 63)
    found = jnp.max(jnp.where(rel == below, 1, 0), axis=1, keepdims=True)
    off = jnp.where(found > 0, below, first)
    offs = jnp.broadcast_to(off, (40, MORT))
    ox = jnp.bitwise_and(offs, 3)
    oy = jnp.bitwise_and(jnp.right_shift(offs, 2), 7)
    oz = jnp.right_shift(offs, 5)

    def y_moves(carry):
        shift = oy + jnp.where(carry, 1, 0)
        short = jnp.bitwise_and(shift, 7)
        short = jnp.where(short > 4, short - 8, short)
        by3 = jnp.where(short >= 2, 1, jnp.where(short <= -2, -1, 0))
        return shift, short - 3 * by3, by3

    shift, a_by1, a_by3 = y_moves(xs < ox)
    _, b_by1, b_by3 = y_moves(xs + ox >= 4)
    flip = jnp.bitwise_and(oz + jnp.where(ys < shift, 1, 0), 1)

    def three(move, ref, up_ref, dn_ref, r):
        return jnp.where(move == 1, up_ref[r], jnp.where(move == -1, dn_ref[r], ref[r]))

    def along_x(ref, r):
        return jnp.where(ox == 0, ref[r], jnp.where(ox == 1, UX[0, r], jnp.where(ox == 2, UX[1, r], UX[2, r])))

    dm = diss[0, 0]
    node = lax.broadcasted_iota(jnp.int32, (64, ELS), 0)

    def ends(i):
        return jnp.where(jnp.bitwise_and(i + 1, 3) < 2, 1.0, 0.0)

    drag = (-3.0 * dm) * (ends(jnp.right_shift(node, 4)) + ends(jnp.right_shift(node, 2)) + ends(node))

    @pl.loop(0, 5)
    def _(g):
        highs, lows = [], []
        for d in range(3):
            mixed = jac[g, d, 0] * X[0:64]
            for h in range(1, 5):
                mixed += jac[g, d, h] * X[64 * h : 64 * h + 64]
            high, low = split(mixed)
            highs.append(high)
            lows.append(low)
        stack = jnp.concatenate(highs + lows + highs, axis=0)
        mine = pl.ds(pl.multiple_of(g * 64, 64), 64)
        ACC[mine] = jnp.dot(dcat[...], stack, preferred_element_type=f32) + drag * X[mine]

    def relay(first_step, last_step):
        @pl.loop(first_step, last_step)
        def _(k):
            for side in range(2):
                mm(side, k).wait_recv()
                r = rows(side, k)
                NS[r] = combine(("no", "np", "k"), (X, XP, MR), side, r)

            @pl.when(k > 0)
            def _():
                for side in range(2):
                    nn(side, jnp.maximum(k - 1, 0)).start()

    arrive([across_hop])
    for r in (lo, hi):
        V[r] = jnp.where(flip == 1, TZ[r], T[r])
    ACC4[0] = jnp.zeros((ROWS, 128), f32)
    begin(b1)
    begin(a1)

    column = lax.broadcasted_iota(jnp.int32, (640, ELS), 0)

    def mix(face, outer, g):
        d, sign = face // 2, (1.0 if face % 2 else -1.0)
        total = (3.0 * dm) * outer[g]
        for h in range(5):
            total -= (3.0 * sign) * jac[g, d, h] * outer[h]
        return total

    def gather_face(face):
        d, end = face // 2, 3 * (face % 2)
        far = 3 - end

        def pick(ref):
            if d == 0:
                return jnp.concatenate([ref[64 * g + 16 * far : 64 * g + 16 * far + 16] for g in range(5)], axis=0)
            t = 8 * (far // 2)
            return jnp.concatenate([ref[16 * a + t : 16 * a + t + 8] for a in range(20)], axis=0)

        if d == 2:
            picked = [X4[j, pl.ds(far, 80, stride=4), :] for j in range(4)] + [H[pl.ds(far, 80, stride=4), :]]
        else:
            picked = [pick(X), pick(H)]
        source = jnp.concatenate(picked, axis=1)
        high, low = split(source)
        k = nb[face : face + 1, :]
        place = jnp.where(k < RIM, k + ELS, jnp.where(k < RIM + ELS, k - RIM, k))
        if face == 5:
            q = lax.broadcasted_iota(jnp.int32, (1, ELS), 1)
            place = jnp.where((q >= 2 * RIM) & (q < 2 * RIM + MORT), -1, place)
        hot = jnp.where(column == place, 1.0, 0.0).astype(bf16)
        both = jnp.dot(jnp.concatenate([high, low], axis=0), hot, preferred_element_type=f32)
        count = source.shape[0]
        got = both[:count] + both[count:]
        per = count // 5
        outer = [got[per * h : per * h + per] for h in range(5)]
        for g in range(5):
            part = mix(face, outer, g)
            if d == 0:
                ACC[64 * g + 16 * end : 64 * g + 16 * end + 16] += part
            elif d == 1:
                sub = lax.broadcasted_iota(jnp.int32, (8, ELS), 0)
                t = 8 * (end // 2)
                keep = (sub >= 4) if end == 3 else (sub < 4)
                for a in range(4):
                    piece = pltpu.roll(part[8 * a : 8 * a + 8], 4, 0)
                    at_row = 64 * g + 16 * a + t
                    ACC[at_row : at_row + 8] += jnp.where(keep, piece, 0.0)
            else:
                for j in range(4):
                    ACC4[j, pl.ds(64 * g + end, 16, stride=4), :] = part[:, 128 * j : 128 * j + 128]

    relay(0, 1)
    halo_a.wait_recv()
    halo_b.wait_recv()
    H[0:160] = jnp.where(lane < 64, RB[...], pltpu.roll(RA[...], 64, 1))
    H[160:320] = jnp.where(lane < 64, pltpu.roll(RB[...], 64, 1), RA[...])
    for j in range(1, 4):
        ACC4[j] = jnp.zeros((ROWS, 128), f32)
    gather_face(0)
    arrive(a1)
    W[lo] = three(a_by1, V, VU, VD, lo)
    gather_face(1)
    begin(a2)
    arrive(b1)
    U[hi] = along_x(V, hi)
    relay(1, 2)
    begin(b2)
    gather_face(2)
    gather_face(3)
    arrive(b2)
    W[hi] = three(b_by1, U, VU, VD, hi)
    gather_face(4)
    begin(b3)
    relay(2, 4)
    arrive(a2)
    U[lo] = three(a_by3, W, WU, WD, lo)
    gather_face(5)
    begin(a3)
    relay(4, STEPS)

    metric = met[...]
    w0 = om[0, 0]
    pace = courant_number / (metric * dm + w0)
    gain = pace * metric
    drop = pace * w0
    live = lax.broadcasted_iota(jnp.int32, (1, ELS), 1) < cnt[0, 0]
    gain = jnp.where(live, gain, 0.0)
    drop = jnp.where(live, drop, 0.0)
    keep = jnp.where(live, 1.0, 0.0)
    for side in range(2):
        nn(side, STEPS - 1).start()
    def face_base():
        @pl.loop(0, STEPS)
        def _(k):
            for side in range(2):
                r = rows(side, k)
                ACC[r] = keep * X[r] + gain * ACC[r] - drop * combine(("bo", "bp", "fm"), (X, XP, MR), side, r)

    turn = jnp.full((16, MORT), ang[0, 0], f32)
    cosine, sine = jnp.cos(turn), jnp.sin(turn)
    index = jnp.bitwise_and(rel - off + 64, 63) * MORT + jnp.bitwise_and(pairs, MORT - 1)
    hot = jnp.where(lax.broadcasted_iota(jnp.int32, (2 * MORT, MORT), 0) == index, 1.0, 0.0).astype(bf16)
    remote(X, XP, ex_s, ex_r.at[0, 0], mate, sp).wait_send()
    for side in range(2):
        mm_sent(side).wait_send()
    arrive(b3)
    Q[hi] = three(b_by3, W, WU, WD, hi)
    face_base()
    begin([last_hi])
    arrive(a3)
    Q[lo] = along_x(U, lo)
    remote(X, XP, c_s.at[0], ex_r.at[0, 0], mate, sp).wait_send()
    remote(H, H, h_s, h_r.at[0], me, prv).wait_send()
    begin([last_lo])

    @pl.loop(0, STEPS)
    def _(k):
        for side in range(2):
            nn(side, k).wait_recv()
            r = rows(side, k)
            ES[r] = combine(("em", "en"), (MR, NR), side, r)

        @pl.when(k > 0)
        def _():
            for side in range(2):
                ee(side, jnp.maximum(k - 1, 0)).start()

    for side in range(2):
        nn_sent(side).wait_send()
    for side in range(2):
        ee(side, STEPS - 1).start()
    arrive([last_hi, last_lo])
    window = jnp.concatenate([Q[...], QN[...]], axis=1)
    high, low = split(window)
    both = jnp.dot(jnp.concatenate([high, low], axis=0), hot, preferred_element_type=f32)
    got = both[:80] + both[80:]
    outer = [got[16 * h : 16 * h + 16] for h in range(5)]
    outer[2], outer[3] = cosine * outer[2] - sine * outer[3], sine * outer[2] + cosine * outer[3]
    for g in range(5):
        part = mix(5, outer, g)
        for j in range(2):
            ACC4[1 + j, pl.ds(64 * g + 3, 16, stride=4), :] += part[:, 128 * j : 128 * j + 128]

    def put(side, k):
        r = rows(side, k)
        return pltpu.make_async_copy(OUT.at[r], out.at[r], out_sem)

    @pl.loop(0, STEPS)
    def _(k):
        for side in range(2):
            ee(1 - side, k).wait_recv()
            r = rows(side, k)
            face = jnp.concatenate([ACC4[j, r] for j in range(4)], axis=1)
            OUT[r] = ACC[r] + gain * face - drop * (coef("fn", side) * NR[r] + ER[r])
            put(side, k).start()

    for side in range(2):
        ee_sent(side).wait_send()

    remote(Q, QN, c_s.at[1], c_r.at[15], me, prv).wait_send()
    pltpu.make_async_copy(OUT, out, out_sem).wait()


def shards(state, metric, jacobians, dissipation, omega, rotor_angle, counts, neighbours, mortar_pairs):
    anywhere = pl.BlockSpec(memory_space=pltpu.HBM)
    whole = pltpu.VMEM((ROWS, ELS), f32)
    quarter = pltpu.VMEM((160, 128), f32)
    trace = pltpu.VMEM((80, MORT), f32)
    sem = pltpu.SemaphoreType.DMA
    operands = [
        state.reshape(ROWS, ELS),
        metric.reshape(1, ELS),
        jnp.transpose(jacobians, (1, 0, 2)),
        dissipation.reshape(1, 1),
        omega.reshape(1, 1),
        rotor_angle.reshape(1, 1),
        counts.reshape(1, 1),
        neighbours,
        mortar_pairs,
        jnp.asarray(node_operator()),
    ]
    operands = [a if a.size == 1 else pltpu.with_memory_space_constraint(a, pltpu.HBM) for a in operands]
    result = pl.pallas_call(
        kernel,
        out_shape=jax.ShapeDtypeStruct((ROWS, ELS), f32),
        in_specs=[pl.BlockSpec(memory_space=pltpu.VMEM) if a.size == 1 else anywhere for a in operands],
        out_specs=pl.BlockSpec(memory_space=pl.ANY),
        scratch_shapes=[whole] * 10
        + [pltpu.VMEM((4, ROWS, 128), f32)] * 2
        + [quarter] * 4
        + [pltpu.VMEM((ROWS, 128), f32)]
        + [trace] * 9
        + [pltpu.VMEM((3, 80, MORT), f32)]
        + [trace] * 2
        + [pltpu.VMEM((1, ELS), f32), pltpu.VMEM((6, ELS), jnp.int32), pltpu.VMEM((1, MORT), jnp.int32)]
        + [pltpu.VMEM((64, 576), bf16), pltpu.SMEM((5, 3, 5), f32)]
        + [pltpu.SMEM((1, 1), f32)] * 3
        + [pltpu.SMEM((1, 1), jnp.int32)]
        + [sem((14,)), sem(()), sem((2, STEPS))]
        + [sem((2,)), sem((2, STEPS))] * 3
        + [sem(()), sem((2,))]
        + [sem((2,)), sem((17,))]
        + [sem(())],
        compiler_params=pltpu.CompilerParams(collective_id=0, has_side_effects=True, vmem_limit_bytes=VMEM_BYTES),
        name="step",
    )(
        *operands,
    )
    return result.reshape(state.shape)


def solution(mesh):
    return jax.shard_map(
        shards,
        mesh=mesh,
        in_specs=(
            P("inst", None, None, "space"),
            P("space"),
            P(),
            P(),
            P(),
            P("inst"),
            P("space"),
            P(None, "space"),
            P("inst", "space"),
        ),
        out_specs=P("inst", None, None, "space"),
        check_vma=False,
    )
```

```python
import functools
import math

import jax
import jax.numpy as jnp
import numpy as np
from jax import lax
from jax.experimental import pallas as pl
from jax.experimental.pallas import tpu as pltpu
from jax.sharding import PartitionSpec as P

RIM = 64
MORT = 256
ROWS = 320
ELS = 512
STEPS = 4
PIECE = ROWS // 2 // STEPS
VMEM_BYTES = 24 * 2**20
MESH = pl.DeviceIdType.MESH
f32 = jnp.float32
bf16 = jnp.bfloat16

courant_number = 0.5


def gll_table():
    nodes = np.array([-1.0, -1.0 / math.sqrt(5.0), 1.0 / math.sqrt(5.0), 1.0])
    barycentric = np.array(
        [1.0 / np.prod([nodes[j] - nodes[k] for k in range(4) if k != j]) for j in range(4)]
    )
    derivative = np.zeros((4, 4))
    for i in range(4):
        for j in range(4):
            if i != j:
                derivative[i, j] = barycentric[j] / barycentric[i] / (nodes[i] - nodes[j])
        derivative[i, i] = -np.sum(derivative[i])
    return derivative


def node_operator():
    along = -gll_table()
    along[0, 0] -= 3.0
    along[3, 3] += 3.0
    eye = np.eye(4)
    full = np.concatenate(
        [
            np.kron(np.kron(along, eye), eye),
            np.kron(np.kron(eye, along), eye),
            np.kron(np.kron(eye, eye), along),
        ],
        axis=1,
    ).astype(np.float32)
    high = full.astype(jnp.bfloat16)
    low = (full - high.astype(np.float32)).astype(jnp.bfloat16)
    return np.concatenate([high, high, low], axis=1)


def spectral_blocks():
    count = 8

    def entry(k):
        k = k % count
        if k == 0:
            return (count * count + 2.0) / (12.0 * count)
        parity = (-1.0) ** k
        angle = math.pi * k / count
        return 0.5 * parity / math.tan(angle) + parity / (2.0 * count * math.sin(angle) ** 2)

    return [np.array([[entry(2 * d + r - s) for s in range(2)] for r in range(2)]) for d in range(4)]


def coding():
    own, near, far, back = spectral_blocks()
    turn = np.array([[0.0, -1.0], [1.0, 0.0]])

    def gap(w):
        a, b = w[:2], w[2:]
        return (near @ turn @ np.outer(a, a) - back @ turn @ np.outer(b, b) - far).ravel()

    w = np.array([0.03903, -0.69895, -1.57892, 0.64467])
    for _ in range(30):
        slope = np.stack([(gap(w + h) - gap(w - h)) / 2e-5 for h in 1e-5 * np.eye(4)], axis=1)
        w = w - np.linalg.solve(slope, gap(w))
    assert np.abs(gap(w)).max() < 1e-12
    sides = []
    for part, block, sign in ((w[:2], near, 1.0), (w[2:], back, -1.0)):
        u = part / np.linalg.norm(part)
        v = turn @ u
        sides.append((u, v, sign * float(part @ part), block @ np.linalg.inv(np.stack([u, v]))))
    table = [[], []]
    for side, (u, v, k, mix) in enumerate(sides):
        for core in range(2):
            table[side].append(dict(
                mo=u[core], mp=u[1 - core], no=v[core], np=v[1 - core], k=k,
                em=mix[1 - core, 0], en=mix[1 - core, 1],
                bo=own[core, core], bp=own[core, 1 - core],
                fm=mix[core, 0], fn=mix[core, 1],
            ))
    return table


def split(value):
    high = value.astype(bf16)
    low = (value - high.astype(f32)).astype(bf16)
    return high, low


def kernel(
    x_hbm, met_hbm, jac_hbm, diss_hbm, om_hbm, ang_hbm, cnt_hbm, nb_hbm, mp_hbm, dcat_hbm, out,
    X, XP, MS, MR, NS, NR, ES, ER, ACC, OUT, X4, ACC4, SA, SB, RA, RB, H,
    T, TZ, V, VU, VD, W, WU, WD, U, UX, Q, QN,
    met, nb, mp, dcat, jac, diss, om, ang, cnt,
    in_sem, ex_s, ex_r, m_s, m_r, n_s, n_r, e_s, e_r, h_s, h_r, c_s, c_r, out_sem,
):
    me = lax.axis_index("inst")
    sp = lax.axis_index("space")
    core = lax.rem(me, 2)
    mate = me + 1 - 2 * core
    up = lax.rem(me + 2, 8)
    down = lax.rem(me + 6, 8)
    xs = lax.rem(sp, 4)
    ys = lax.rem(sp // 4, 8)
    zs = sp // 32
    nxt = lax.rem(sp + 1, 64)
    prv = lax.rem(sp + 63, 64)

    def at(z, y, x):
        return z * 32 + lax.rem(y + 8, 8) * 4 + lax.rem(x + 4, 4)

    across = at(1 - zs, ys, xs)
    y_up, y_dn = at(zs, ys + 1, xs), at(zs, ys - 1, xs)
    y_up3, y_dn3 = at(zs, ys + 3, xs), at(zs, ys - 3, xs)
    x_other = [at(zs, ys, xs + s) for s in (1, 2, 3)]

    def to(i, s):
        return {"inst": i, "space": s}

    barrier = pltpu.get_barrier_semaphore()
    peers = [(mate, sp), (up, sp), (down, sp)]
    peers += [(me, s) for s in (nxt, prv, across, y_up, y_dn, y_up3, y_dn3, *x_other)]
    for i, s in peers:
        pl.semaphore_signal(barrier, inc=1, device_id=to(i, s), device_id_type=MESH)
    pairs_in = [(x_hbm.at[:, 128 * j : 128 * j + 128], X4.at[j]) for j in (1, 2)]
    pairs_in += [(x_hbm, X)]
    pairs_in += [(x_hbm.at[:, 128 * j : 128 * j + 128], X4.at[j]) for j in (0, 3)]
    pairs_in += [
        (jac_hbm, jac), (diss_hbm, diss), (mp_hbm, mp), (dcat_hbm, dcat), (nb_hbm, nb),
        (om_hbm, om), (ang_hbm, ang), (cnt_hbm, cnt), (met_hbm, met),
    ]
    loads = [pltpu.make_async_copy(a, b, in_sem.at[j]) for j, (a, b) in enumerate(pairs_in)]
    for copy in loads:
        copy.start()
    for j in range(2):
        loads[j].wait()
    for j in range(2):
        T[:, 128 * j : 128 * j + 128] = X4[1 + j, pl.ds(0, 80, stride=4), :]

    def remote(src, dst, ss, rs, i, s):
        return pltpu.make_async_remote_copy(
            src_ref=src, dst_ref=dst, send_sem=ss, recv_sem=rs, device_id=to(i, s), device_id_type=MESH
        )

    def half(side):
        return jnp.bitwise_xor(core, side) * (ROWS // 2)

    def rows(side, k):
        return pl.ds(pl.multiple_of(half(side) + k * PIECE, PIECE), PIECE)

    def flow(a, b, ss, rs, device):
        def piece(side, k):
            r = rows(side, k)
            target = mate if device is None else device[side]
            return remote(a.at[r], b.at[r], ss.at[side], rs.at[side, k], target, sp)

        def all_sent(side):
            r = pl.ds(pl.multiple_of(half(side), PIECE), ROWS // 2)
            target = mate if device is None else device[side]
            return remote(a.at[r], b.at[r], ss.at[side], rs.at[side, 0], target, sp)

        return piece, all_sent

    def plain(k, h):
        return pl.ds(pl.multiple_of(h * (ROWS // 2) + k * PIECE, PIECE), PIECE)

    def ex(h, k):
        r = plain(k, h)
        return remote(x_hbm.at[r], XP.at[r], ex_s, ex_r.at[h, k], mate, sp)

    mm, mm_sent = flow(MS, MR, m_s, m_r, (up, down))
    nn, nn_sent = flow(NS, NR, n_s, n_r, (up, down))
    ee, ee_sent = flow(ES, ER, e_s, e_r, None)

    def stage(src, dst, slot, s):
        return remote(src, dst, c_s.at[slot // 15], c_r.at[slot], me, s)

    lo, hi = pl.ds(0, 40), pl.ds(40, 40)

    def ring(src, up_dst, dn_dst, slot, r, u, d):
        return [stage(src.at[r], dn_dst.at[r], slot, u), stage(src.at[r], up_dst.at[r], slot + 1, d)]

    def spread(src, slot, r):
        return [stage(src.at[r], UX.at[j, r], slot + j, x_other[2 - j]) for j in range(3)]

    across_hop = stage(T, TZ, 0, across)
    a1, a2 = ring(V, VU, VD, 1, lo, y_up, y_dn), ring(W, WU, WD, 3, lo, y_up3, y_dn3)
    a3 = spread(U, 5, lo)
    b1 = spread(V, 8, hi)
    b2, b3 = ring(U, VU, VD, 11, hi, y_up, y_dn), ring(W, WU, WD, 13, hi, y_up3, y_dn3)
    last_lo = stage(Q.at[lo], QN.at[lo], 15, prv)
    last_hi = stage(Q.at[hi], QN.at[hi], 16, prv)

    def begin(copies):
        for copy in copies:
            copy.start()

    def arrive(copies):
        for copy in copies:
            copy.wait_recv()

    halo_a = remote(SA, RA, h_s, h_r.at[0], me, prv)
    halo_b = remote(SB, RB, h_s, h_r.at[1], me, nxt)

    pl.semaphore_wait(barrier, len(peers))
    across_hop.start()

    @pl.loop(0, STEPS)
    def _(k):
        for h in range(2):
            ex(h, k).start()

    for copy in loads[2:]:
        copy.wait()

    table = coding()

    def coef(name, side):
        return jnp.where(core == 0, f32(table[side][0][name]), f32(table[side][1][name]))

    def combine(names, parts, side, r):
        total = coef(names[0], side) * parts[0][r]
        for name, ref in zip(names[1:], parts[1:]):
            total += coef(name, side) * ref[r]
        return total

    @pl.loop(0, STEPS)
    def _(k):
        for h in range(2):
            ex(h, k).wait_recv()
        for side in range(2):
            r = rows(side, k)
            MS[r] = combine(("mo", "mp"), (X, XP), side, r)

        @pl.when(k > 0)
        def _():
            for side in range(2):
                mm(side, jnp.maximum(k - 1, 0)).start()

    lane = lax.broadcasted_iota(jnp.int32, (160, 128), 1)
    top, low = X4[0, 0:160], X4[0, 160:320]
    SA[...] = jnp.where(lane < 64, top, pltpu.roll(low, 64, 1))
    SB[...] = jnp.where(lane < 64, pltpu.roll(top, 64, 1), low)
    for side in range(2):
        mm(side, STEPS - 1).start()
    halo_a.start()
    halo_b.start()

    pairs = mp[...]
    rel = jnp.bitwise_and(jnp.right_shift(pairs, 8) - sp + 64, 63)
    first = rel[:, 0:1]
    below = jnp.bitwise_and(first + 63, 63)
    found = jnp.max(jnp.where(rel == below, 1, 0), axis=1, keepdims=True)
    off = jnp.where(found > 0, below, first)
    offs = jnp.broadcast_to(off, (40, MORT))
    ox = jnp.bitwise_and(offs, 3)
    oy = jnp.bitwise_and(jnp.right_shift(offs, 2), 7)
    oz = jnp.right_shift(offs, 5)

    def y_moves(carry):
        shift = oy + jnp.where(carry, 1, 0)
        short = jnp.bitwise_and(shift, 7)
        short = jnp.where(short > 4, short - 8, short)
        by3 = jnp.where(short >= 2, 1, jnp.where(short <= -2, -1, 0))
        return shift, short - 3 * by3, by3

    shift, a_by1, a_by3 = y_moves(xs < ox)
    _, b_by1, b_by3 = y_moves(xs + ox >= 4)
    flip = jnp.bitwise_and(oz + jnp.where(ys < shift, 1, 0), 1)

    def three(move, ref, up_ref, dn_ref, r):
        return jnp.where(move == 1, up_ref[r], jnp.where(move == -1, dn_ref[r], ref[r]))

    def along_x(ref, r):
        return jnp.where(ox == 0, ref[r], jnp.where(ox == 1, UX[0, r], jnp.where(ox == 2, UX[1, r], UX[2, r])))

    dm = diss[0, 0]
    node = lax.broadcasted_iota(jnp.int32, (64, ELS), 0)

    def ends(i):
        return jnp.where(jnp.bitwise_and(i + 1, 3) < 2, 1.0, 0.0)

    drag = (-3.0 * dm) * (ends(jnp.right_shift(node, 4)) + ends(jnp.right_shift(node, 2)) + ends(node))

    @pl.loop(0, 5)
    def _(g):
        highs, lows = [], []
        for d in range(3):
            mixed = jac[g, d, 0] * X[0:64]
            for h in range(1, 5):
                mixed += jac[g, d, h] * X[64 * h : 64 * h + 64]
            high, low = split(mixed)
            highs.append(high)
            lows.append(low)
        stack = jnp.concatenate(highs + lows + highs, axis=0)
        mine = pl.ds(pl.multiple_of(g * 64, 64), 64)
        ACC[mine] = jnp.dot(dcat[...], stack, preferred_element_type=f32) + drag * X[mine]

    def relay(first_step, last_step):
        @pl.loop(first_step, last_step)
        def _(k):
            for side in range(2):
                mm(side, k).wait_recv()
                r = rows(side, k)
                NS[r] = combine(("no", "np", "k"), (X, XP, MR), side, r)

            @pl.when(k > 0)
            def _():
                for side in range(2):
                    nn(side, jnp.maximum(k - 1, 0)).start()

    arrive([across_hop])
    for r in (lo, hi):
        V[r] = jnp.where(flip == 1, TZ[r], T[r])
    ACC4[0] = jnp.zeros((ROWS, 128), f32)
    begin(b1)
    begin(a1)

    column = lax.broadcasted_iota(jnp.int32, (640, ELS), 0)

    def mix(face, outer, g):
        d, sign = face // 2, (1.0 if face % 2 else -1.0)
        total = (3.0 * dm) * outer[g]
        for h in range(5):
            total -= (3.0 * sign) * jac[g, d, h] * outer[h]
        return total

    def gather_face(face):
        d, end = face // 2, 3 * (face % 2)
        far = 3 - end

        def pick(ref):
            if d == 0:
                return jnp.concatenate([ref[64 * g + 16 * far : 64 * g + 16 * far + 16] for g in range(5)], axis=0)
            t = 8 * (far // 2)
            return jnp.concatenate([ref[16 * a + t : 16 * a + t + 8] for a in range(20)], axis=0)

        if d == 2:
            picked = [X4[j, pl.ds(far, 80, stride=4), :] for j in range(4)] + [H[pl.ds(far, 80, stride=4), :]]
        else:
            picked = [pick(X), pick(H)]
        source = jnp.concatenate(picked, axis=1)
        high, low = split(source)
        k = nb[face : face + 1, :]
        place = jnp.where(k < RIM, k + ELS, jnp.where(k < RIM + ELS, k - RIM, k))
        if face == 5:
            q = lax.broadcasted_iota(jnp.int32, (1, ELS), 1)
            place = jnp.where((q >= 2 * RIM) & (q < 2 * RIM + MORT), -1, place)
        hot = jnp.where(column == place, 1.0, 0.0).astype(bf16)
        both = jnp.dot(jnp.concatenate([high, low], axis=0), hot, preferred_element_type=f32)
        count = source.shape[0]
        got = both[:count] + both[count:]
        per = count // 5
        outer = [got[per * h : per * h + per] for h in range(5)]
        for g in range(5):
            part = mix(face, outer, g)
            if d == 0:
                ACC[64 * g + 16 * end : 64 * g + 16 * end + 16] += part
            elif d == 1:
                sub = lax.broadcasted_iota(jnp.int32, (8, ELS), 0)
                t = 8 * (end // 2)
                keep = (sub >= 4) if end == 3 else (sub < 4)
                for a in range(4):
                    piece = pltpu.roll(part[8 * a : 8 * a + 8], 4, 0)
                    at_row = 64 * g + 16 * a + t
                    ACC[at_row : at_row + 8] += jnp.where(keep, piece, 0.0)
            else:
                for j in range(4):
                    ACC4[j, pl.ds(64 * g + end, 16, stride=4), :] = part[:, 128 * j : 128 * j + 128]

    halo_a.wait_recv()
    halo_b.wait_recv()
    H[0:160] = jnp.where(lane < 64, RB[...], pltpu.roll(RA[...], 64, 1))
    H[160:320] = jnp.where(lane < 64, pltpu.roll(RB[...], 64, 1), RA[...])
    for j in range(1, 4):
        ACC4[j] = jnp.zeros((ROWS, 128), f32)
    gather_face(0)
    arrive(a1)
    W[lo] = three(a_by1, V, VU, VD, lo)
    gather_face(1)
    begin(a2)
    arrive(b1)
    U[hi] = along_x(V, hi)
    begin(b2)
    relay(0, 2)
    gather_face(2)
    gather_face(3)
    arrive(b2)
    W[hi] = three(b_by1, U, VU, VD, hi)
    gather_face(4)
    begin(b3)
    relay(2, 3)
    arrive(a2)
    U[lo] = three(a_by3, W, WU, WD, lo)
    gather_face(5)
    begin(a3)
    relay(3, STEPS)

    metric = met[...]
    w0 = om[0, 0]
    pace = courant_number / (metric * dm + w0)
    gain = pace * metric
    drop = pace * w0
    live = lax.broadcasted_iota(jnp.int32, (1, ELS), 1) < cnt[0, 0]
    gain = jnp.where(live, gain, 0.0)
    drop = jnp.where(live, drop, 0.0)
    keep = jnp.where(live, 1.0, 0.0)
    for side in range(2):
        nn(side, STEPS - 1).start()
    def face_base():
        @pl.loop(0, STEPS)
        def _(k):
            for side in range(2):
                r = rows(side, k)
                ACC[r] = keep * X[r] + gain * ACC[r] - drop * combine(("bo", "bp", "fm"), (X, XP, MR), side, r)

    turn = jnp.full((16, MORT), ang[0, 0], f32)
    cosine, sine = jnp.cos(turn), jnp.sin(turn)
    index = jnp.bitwise_and(rel - off + 64, 63) * MORT + jnp.bitwise_and(pairs, MORT - 1)
    hot = jnp.where(lax.broadcasted_iota(jnp.int32, (2 * MORT, MORT), 0) == index, 1.0, 0.0).astype(bf16)
    remote(x_hbm, XP, ex_s, ex_r.at[0, 0], mate, sp).wait_send()
    for side in range(2):
        mm_sent(side).wait_send()
    arrive(b3)
    Q[hi] = three(b_by3, W, WU, WD, hi)
    face_base()
    begin([last_hi])
    arrive(a3)
    Q[lo] = along_x(U, lo)
    remote(X, XP, c_s.at[0], ex_r.at[0, 0], mate, sp).wait_send()
    remote(H, H, h_s, h_r.at[0], me, prv).wait_send()
    begin([last_lo])

    @pl.loop(0, STEPS)
    def _(k):
        for side in range(2):
            nn(side, k).wait_recv()
            r = rows(side, k)
            ES[r] = combine(("em", "en"), (MR, NR), side, r)

        @pl.when(k > 0)
        def _():
            for side in range(2):
                ee(side, jnp.maximum(k - 1, 0)).start()

    for side in range(2):
        nn_sent(side).wait_send()
    for side in range(2):
        ee(side, STEPS - 1).start()
    arrive([last_hi, last_lo])
    window = jnp.concatenate([Q[...], QN[...]], axis=1)
    high, low = split(window)
    both = jnp.dot(jnp.concatenate([high, low], axis=0), hot, preferred_element_type=f32)
    got = both[:80] + both[80:]
    outer = [got[16 * h : 16 * h + 16] for h in range(5)]
    outer[2], outer[3] = cosine * outer[2] - sine * outer[3], sine * outer[2] + cosine * outer[3]
    for g in range(5):
        part = mix(5, outer, g)
        for j in range(2):
            ACC4[1 + j, pl.ds(64 * g + 3, 16, stride=4), :] += part[:, 128 * j : 128 * j + 128]

    def put(side, k):
        r = rows(side, k)
        return pltpu.make_async_copy(OUT.at[r], out.at[r], out_sem)

    @pl.loop(0, STEPS)
    def _(k):
        for side in range(2):
            ee(1 - side, k).wait_recv()
            r = rows(side, k)
            face = jnp.concatenate([ACC4[j, r] for j in range(4)], axis=1)
            OUT[r] = ACC[r] + gain * face - drop * (coef("fn", side) * NR[r] + ER[r])
            put(side, k).start()

    for side in range(2):
        ee_sent(side).wait_send()

    remote(Q, QN, c_s.at[1], c_r.at[15], me, prv).wait_send()
    pltpu.make_async_copy(OUT, out, out_sem).wait()


def shards(state, metric, jacobians, dissipation, omega, rotor_angle, counts, neighbours, mortar_pairs):
    anywhere = pl.BlockSpec(memory_space=pltpu.HBM)
    whole = pltpu.VMEM((ROWS, ELS), f32)
    quarter = pltpu.VMEM((160, 128), f32)
    trace = pltpu.VMEM((80, MORT), f32)
    sem = pltpu.SemaphoreType.DMA
    operands = [
        state.reshape(ROWS, ELS),
        metric.reshape(1, ELS),
        jnp.transpose(jacobians, (1, 0, 2)),
        dissipation.reshape(1, 1),
        omega.reshape(1, 1),
        rotor_angle.reshape(1, 1),
        counts.reshape(1, 1),
        neighbours,
        mortar_pairs,
        jnp.asarray(node_operator()),
    ]
    operands = [a if a.size == 1 else pltpu.with_memory_space_constraint(a, pltpu.HBM) for a in operands]
    result = pl.pallas_call(
        kernel,
        out_shape=jax.ShapeDtypeStruct((ROWS, ELS), f32),
        in_specs=[pl.BlockSpec(memory_space=pltpu.VMEM) if a.size == 1 else anywhere for a in operands],
        out_specs=pl.BlockSpec(memory_space=pl.ANY),
        scratch_shapes=[whole] * 10
        + [pltpu.VMEM((4, ROWS, 128), f32)] * 2
        + [quarter] * 4
        + [pltpu.VMEM((ROWS, 128), f32)]
        + [trace] * 9
        + [pltpu.VMEM((3, 80, MORT), f32)]
        + [trace] * 2
        + [pltpu.VMEM((1, ELS), f32), pltpu.VMEM((6, ELS), jnp.int32), pltpu.VMEM((1, MORT), jnp.int32)]
        + [pltpu.VMEM((64, 576), bf16), pltpu.SMEM((5, 3, 5), f32)]
        + [pltpu.SMEM((1, 1), f32)] * 3
        + [pltpu.SMEM((1, 1), jnp.int32)]
        + [sem((14,)), sem(()), sem((2, STEPS))]
        + [sem((2,)), sem((2, STEPS))] * 3
        + [sem(()), sem((2,))]
        + [sem((2,)), sem((17,))]
        + [sem(())],
        compiler_params=pltpu.CompilerParams(collective_id=0, has_side_effects=True, vmem_limit_bytes=VMEM_BYTES),
        name="step",
    )(
        *operands,
    )
    return result.reshape(state.shape)


def solution(mesh):
    return jax.shard_map(
        shards,
        mesh=mesh,
        in_specs=(
            P("inst", None, None, "space"),
            P("space"),
            P(),
            P(),
            P(),
            P("inst"),
            P("space"),
            P(None, "space"),
            P("inst", "space"),
        ),
        out_specs=P("inst", None, None, "space"),
        check_vma=False,
    )
```
